32 devices in a mesh: gx: 2 (over x), gy: 4 (over y, core), gz: 4 (over z).
Axes of the slice: x: 2, y: 2, z: 4, core: 2. Of those that a mesh axis runs over, the one named last changes fastest.
Arguments:
- offset: float32 [3, 8, 2, 16, 512], P(None, None, 'gx', 'gy', 'gz'), may hold values from 0.05 to 0.95, as said below
- velocity: float32 [3, 8, 2, 16, 512], P(None, None, 'gx', 'gy', 'gz'), may hold values from -11 to 11
- occupancy: int32 [2, 16, 512], P('gx', 'gy', 'gz'), may hold values from 1 to 8
- noise: bfloat16 [14, 8, 8, 2, 16, 512], P(None, None, None, 'gx', 'gy', 'gz'), may hold values from -4 to 4
Outputs:
- interaction_push_per_bead: float32 [3, 8, 2, 16, 512], P(None, None, 'gx', 'gy', 'gz')
- stress_matrix: float32 [3, 3], replicated
- thermal_level: float32 [1], replicated
The draws below stay inside these ranges and needn't reach their ends.
Inputs may be any that keep to these rules, and one draw needn't show every extreme that they name: `offset`: two beads of the grid are never closer than 0.1. `occupancy`: at most 8 beads a cell, in its first slots.
All inputs are finite; a program needn't handle non-finite values.
Results may differ from the reference program's by a relative error of at most 0.0003.
Values may be sent and summed in bfloat16 or wider, within the bound.
A program may use at most 64 MiB of HBM per device.

```python
from functools import partial
import jax
import jax.numpy as jnp
from jax import lax

P_SIZE = 8
NX = 2
NY = 16
NZ = 512


def draw_offset(key, part):
    shape = (3, P_SIZE, NX, NY, NZ)
    comp = lax.broadcasted_iota(jnp.int32, shape, 0)
    slot = lax.broadcasted_iota(jnp.int32, shape, 1)
    half = (slot // 2 ** comp % 2).astype(jnp.float32)
    base = jax.random.uniform(key, shape, jnp.float32)
    random_kick = 0.05 + 0.4 * base
    return 0.5 * half + random_kick


def draw_velocity(key, part):
    shape = (3, P_SIZE, NX, NY, NZ)
    xpos = lax.broadcasted_iota(jnp.int32, shape, 2).astype(jnp.float32)
    ypos = lax.broadcasted_iota(jnp.int32, shape, 3).astype(jnp.float32)
    zpos = lax.broadcasted_iota(jnp.int32, shape, 4).astype(jnp.float32)
    heat = 0.25 * (1.0 + 2.0 * xpos / NX) * (1.0 + 2.0 * ypos / NY) * (1.0 + 2.0 * zpos / NZ)
    raw = jax.random.truncated_normal(key, -4.0, 4.0, shape, jnp.float32)
    return raw * jnp.sqrt(heat)


def with_ends(result, key, low, high):
    longest = result.shape.index(max(result.shape))
    spots = []
    for shift in (0, 1):
        where = [jax.random.randint(jax.random.fold_in(key, axis), (), 0, length) for axis, length in enumerate(result.shape)]
        where[longest] = (where[longest] + shift) % result.shape[longest]
        spots.append(tuple(where))
    return result.at[spots[0]].set(low).at[spots[1]].set(high)


def block_scale(own_key, extent, split, low, high):
    def one(position, blocks):
        draws = jax.random.uniform(jax.random.fold_in(jax.random.fold_in(own_key, 6), position), (blocks,), jnp.float32, low / len(split), high / len(split))
        return jnp.repeat(jnp.exp(draws), extent[position] // blocks).reshape((-1,) + (1,) * (len(extent) - position - 1))

    level = one(*split[0])
    for cut in split[1:]:
        level = level * one(*cut)
    return level


def bell_draw(stream_key, shape, scale, reach, pieces=(), held_as=jnp.bfloat16):
    entries = scale * jax.random.normal(stream_key, shape, jnp.float32)
    if pieces:
        entries = entries * block_scale(stream_key, shape, pieces, -0.22, 0.18)
    return jnp.clip(entries, -reach, reach).astype(held_as)


def setup_inputs(seed: int = 0) -> dict:
    seeds = jax.random.split(jax.random.key(seed), 5)
    return {
        "offset": draw_offset(jax.random.fold_in(seeds[4], 71), 0),
        "velocity": draw_velocity(jax.random.fold_in(seeds[4], 71), 0),
        "occupancy": with_ends(jax.random.randint(seeds[2], (NX, NY, NZ), 1, P_SIZE + 1), jax.random.fold_in(seeds[2], 1), 1, P_SIZE).astype(jnp.int32),
        "noise": bell_draw(seeds[3], (14, P_SIZE, P_SIZE, NX, NY, NZ), 1.0, 4.0, ((3, 2), (4, 4), (5, 4))),
    }


REPULSION = 25.0
FRICTION = 4.5
NOISE_SCALE = 15.0
forward_shifts = [(1, 0, 0), (-1, 1, 0), (0, 1, 0), (1, 1, 0)] + [(dx, dy, 1) for dy in (-1, 0, 1) for dx in (-1, 0, 1)]

def outer_total(left, right):
    product = left[:, None] * right[None, :]
    return lax.optimization_barrier(jnp.sum(product.reshape(3, 3, -1), axis=2))

def pair_tile(own, other, theta, shift_vec, identical_couple):
    extra = (1,) * (own.ndim - 2)
    slots = own.shape[1]
    dvec = jnp.array(shift_vec, dtype=jnp.float32).reshape((3, 1, 1) + extra)
    sep = own[0:3, :, None] - other[0:3, None, :] - dvec
    rel_vel = own[3:6, :, None] - other[3:6, None, :]
    live = own[6][:, None] * other[6][None, :]
    dist2 = lax.optimization_barrier(jnp.sum(sep * sep, axis=0))
    if identical_couple:
        same = (lax.broadcasted_iota(jnp.int32, (slots, slots), 0) == lax.broadcasted_iota(jnp.int32, (slots, slots), 1)).astype(jnp.float32).reshape((slots, slots) + extra)
        dist2 = dist2 + same
        live = live * (1.0 - same)
    dist = jnp.sqrt(dist2)
    weight = jnp.maximum(1.0 - dist, 0.0)
    unit = sep / dist
    closing_speed = lax.optimization_barrier(jnp.sum(unit * rel_vel, axis=0))
    force_magnitude = live * weight * (REPULSION - FRICTION * weight * closing_speed + NOISE_SCALE * theta)
    force = force_magnitude * unit
    clausius_moment = outer_total(sep, force)
    return (force, clausius_moment)

def plane_forces(args, shift_vec, identical_couple):
    own, other, theta = args
    force, clausius_moment = pair_tile(own, other, theta, shift_vec, identical_couple)
    return (lax.optimization_barrier(jnp.sum(force, axis=2)), lax.optimization_barrier(jnp.sum(force, axis=1)), clausius_moment)

def reference(offset, velocity, occupancy, noise):
    slots = offset.shape[1]
    live = (lax.broadcasted_iota(jnp.int32, (slots,) + occupancy.shape, 0) < occupancy[None]).astype(jnp.float32)
    pack = jnp.concatenate([offset, velocity, live[None]], axis=0)
    own_planes = jnp.moveaxis(pack, 2, 0)
    theta0 = noise[0].astype(jnp.float32)
    theta0 = (theta0 + jnp.swapaxes(theta0, 0, 1)) * 0.7071067811865476
    acting_upon_itself, unused, vir_self = lax.map(partial(plane_forces, shift_vec=(0, 0, 0), identical_couple=True), (own_planes, own_planes, jnp.moveaxis(theta0, 2, 0)))
    interaction_push_per_bead = jnp.moveaxis(acting_upon_itself, 0, 2)
    clausius_moment = 0.5 * lax.optimization_barrier(jnp.sum(vir_self, axis=0))
    for index, shift_vec in enumerate(forward_shifts):
        dx, dy, dz = shift_vec
        other = jnp.roll(pack, (-dx, -dy, -dz), axis=(2, 3, 4))
        theta = noise[index + 1].astype(jnp.float32)
        on_own, force_on_partner, vir = lax.map(partial(plane_forces, shift_vec=shift_vec, identical_couple=False), (own_planes, jnp.moveaxis(other, 2, 0), jnp.moveaxis(theta, 2, 0)))
        interaction_push_per_bead = interaction_push_per_bead + jnp.moveaxis(on_own, 0, 2)
        interaction_push_per_bead = interaction_push_per_bead - jnp.roll(jnp.moveaxis(force_on_partner, 0, 2), (dx, dy, dz), axis=(2, 3, 4))
        clausius_moment = clausius_moment + lax.optimization_barrier(jnp.sum(vir, axis=0))
    motion_work_sum = outer_total(velocity * live[None], velocity)
    couple_tally = jnp.sum(live)
    stress_matrix = (motion_work_sum + clausius_moment) / (NX * NY * NZ)
    thermal_level = jnp.reshape((motion_work_sum[0, 0] + motion_work_sum[1, 1] + motion_work_sum[2, 2]) / (3.0 * couple_tally - 3.0), (1,))
    return (interaction_push_per_bead, stress_matrix, thermal_level)
```

```python
import functools
import jax
import jax.numpy as jnp
from jax import lax
from jax.experimental import pallas as pl
from jax.experimental.pallas import tpu as pltpu
from jax.sharding import PartitionSpec as P

REPULSION = 25.0
FRICTION = 4.5
NOISE_SCALE = 15.0
FAR = 64.0
PAIRS = ((0, 0), (0, 1), (0, 2), (1, 1), (1, 2), (2, 2))
forward_shifts = [(1, 0, 0), (-1, 1, 0), (0, 1, 0), (1, 1, 0)] + [
    (dx, dy, 1) for dy in (-1, 0, 1) for dx in (-1, 0, 1)
]
MESH = pl.DeviceIdType.MESH


def tiles_of(dx):
    return [(k + 1, d) for k, d in enumerate(forward_shifts) if d[0] == dx]


def groups_of(nx):
    if nx == 2:
        return [(0, (0,)), (1, (1, -1))]
    return [(0, (0,)), (1, (1,)), (-1, (-1,))]


def kernel(
    sizes, slots, Y,
    off_ref, vel_ref, occ_ref, noise_ref,
    push_ref, stress_ref, thermal_ref,
    nz, n0, own, V, ysend, yrecv, Gy, csend, crecv, oth, Bs, accA, vacc,
    R, Rrecv, Gacc, RGsend, RGrecv, RCsend, RCrecv, stat, statxy, statp, statz,
    nsem, ssem, rsem,
):
    nx, ny, nz_dev = sizes
    rows = slots * Y
    Z = off_ref.shape[2]
    G = 8 // Y
    nv = rows // 8
    groups = groups_of(nx)
    ng = len(groups)
    me = (lax.axis_index("gx"), lax.axis_index("gy"), lax.axis_index("gz"))

    def dev(e):
        return tuple(lax.rem(m + (o % n), n) for m, o, n in zip(me, e, sizes))

    noise_copy = pltpu.make_async_copy(noise_ref, nz, nsem)
    noise_copy.start()

    partners = set()
    for ex, _ in groups:
        for ey in (-1, 0, 1):
            for ez in (-1, 0, 1):
                partners.add((ex % nx, ey % ny, ez % nz_dev))
                partners.add((-ex % nx, ey % ny, ez % nz_dev))
    for ex in range(nx):
        for ey in range(ny):
            partners.add((ex, ey, 0))
    for ez in range(nz_dev):
        partners.add((0, 0, ez))
    partners.discard((0, 0, 0))
    partners = sorted(partners)
    barrier = pltpu.get_barrier_semaphore()
    for e in partners:
        pl.semaphore_signal(barrier, inc=1, device_id=dev(e), device_id_type=MESH)

    lane = lax.broadcasted_iota(jnp.int32, (8, Z), 1)
    row = lax.broadcasted_iota(jnp.int32, (8, Z), 0)
    row_y = lax.rem(row, Y)
    lane_f = lax.broadcasted_iota(jnp.int32, (rows, Z), 1)
    row_f = lax.broadcasted_iota(jnp.int32, (rows, Z), 0)
    rowy_f = lax.rem(row_f, Y)
    slot_f = row_f // Y

    occ = occ_ref[...]
    occ8 = jnp.concatenate([occ] * G, axis=0)
    occ_f = jnp.concatenate([occ8] * nv, axis=0)
    live_f = slot_f < occ_f
    for c in range(3):
        x = off_ref[c]
        if c == 0:
            V[0, 0] = jnp.where(live_f, x, FAR)
        else:
            V[0, c] = x
        V[0, 3 + c] = vel_ref[c] * FRICTION
    for s in range(slots):
        for c in range(3):
            x = off_ref[c, pl.ds(s * Y, Y), :]
            x = jnp.concatenate([x] * G, axis=0)
            if c == 0:
                x = jnp.where(occ8 > s, x, -FAR)
            own[s, c] = x
            v = vel_ref[c, pl.ds(s * Y, Y), :] * FRICTION
            own[s, 3 + c] = jnp.concatenate([v] * G, axis=0)
    compact = jnp.zeros((8, Z), jnp.float32)
    for c in range(6):
        ysend[0, c] = V[0, c, pl.ds(Y - 1, slots, stride=Y), :]
        ysend[1, c] = V[0, c, pl.ds(0, slots, stride=Y), :]
        for v in range(nv):
            i = c * nv + v
            x = V[0, c, pl.ds(v * 8, 8), :]
            compact = jnp.where(lane == i, pltpu.roll(x, i, 1) if i else x, compact)
    csend[...] = compact

    def fold(x):
        total = x[0:8]
        for v in range(1, nv):
            total = total + x[v * 8 : v * 8 + 8]
        return total

    vels = [jnp.where(live_f, vel_ref[c], 0.0) for c in range(3)]
    for q, (a, b) in enumerate(PAIRS):
        stat[pl.ds(6 + q, 1), :] = jnp.sum(fold(vels[a] * vels[b]), axis=0, keepdims=True)
    stat[pl.ds(12, 1), :] = jnp.sum(fold(live_f.astype(jnp.float32)), axis=0, keepdims=True)
    stat[pl.ds(13, 3), :] = jnp.zeros((3, Z), jnp.float32)
    accA[...] = jnp.zeros(accA.shape, jnp.float32)
    vacc[...] = jnp.zeros(vacc.shape, jnp.float32)

    def pair_rows(j, h, theta_of, self_tile):
        base = pl.multiple_of(h * 16, 16)
        src = V if self_tile else oth
        other = [src[j, c, pl.ds(base, 16), :].reshape(2, 8, Z) for c in range(6)]
        B = [jnp.zeros((2, 8, Z), jnp.float32) for _ in range(3)]
        for s in range(slots):
            theta = theta_of(s, base).reshape(2, 8, Z)
            mine = [own[s, c] for c in range(6)]
            sep = [mine[c][None] - other[c] for c in range(3)]
            rel = [mine[3 + c][None] - other[3 + c] for c in range(3)]
            dist2 = sep[0] * sep[0] + sep[1] * sep[1] + sep[2] * sep[2]
            if self_tile:
                pos = lax.broadcasted_iota(jnp.int32, (2, 8, Z), 0) * 8
                pos = pos + lax.broadcasted_iota(jnp.int32, (2, 8, Z), 1) + h * 16
                dist2 = jnp.where(pos // Y == s, 4.0, dist2)
            inv = lax.rsqrt(dist2)
            w = jnp.maximum(1.0 - dist2 * inv, 0.0)
            closing = (sep[0] * rel[0] + sep[1] * rel[1] + sep[2] * rel[2]) * inv
            f = w * (REPULSION + NOISE_SCALE * theta - w * closing) * inv
            for c in range(3):
                F = f * sep[c]
                if not self_tile:
                    B[c] = B[c] + F
                accA[s, c] = accA[s, c] + (F[0] + F[1])
        if not self_tile:
            for c in range(3):
                Bs[j, c, pl.ds(base, 16), :] = B[c].reshape(16, Z)
            for q, (a, b) in enumerate(PAIRS):
                m = other[a] * B[b]
                vacc[q] = vacc[q] - (m[0] + m[1])

    noise_copy.wait()
    for t in range(slots):
        x = nz[0, t].astype(jnp.float32)
        for s in range(slots):
            n0[s, pl.ds(t * Y, Y), :] = x[s * Y : s * Y + Y]

    def self_loop(h, carry):
        def theta_of(s, base):
            straight = nz[0, s, pl.ds(base, 16), :].astype(jnp.float32)
            return (straight + n0[s, pl.ds(base, 16), :]) * 0.7071067811865476

        pair_rows(0, h, theta_of, True)
        return carry

    lax.fori_loop(0, rows // 16, self_loop, 0)

    pl.semaphore_wait(barrier, len(partners))

    count = [0]

    def send(src, dst, e):
        i = count[0]
        count[0] += 1
        copy = pltpu.make_async_remote_copy(
            src_ref=src, dst_ref=dst, send_sem=ssem.at[i], recv_sem=rsem.at[i],
            device_id=dev(e), device_id_type=MESH,
        )
        copy.start()
        return copy

    every = []
    halo = {}
    for g, (ex, _) in enumerate(groups):
        halo[g] = [
            send(ysend.at[1], yrecv.at[g, 1], (-ex, -1, 0)),
            send(ysend.at[0], yrecv.at[g, 0], (-ex, 1, 0)),
        ]
        for e in (-1, 0, 1):
            halo[g].append(send(csend, crecv.at[g, e + 1], (-ex, -e, -1)))
        if g == 0:
            for g2, (ex2, _) in enumerate(groups):
                if g2:
                    halo[-g2] = [send(V.at[0], V.at[g2], (-ex2, 0, 0))]
        every += halo[g]
    for g in range(1, ng):
        every += halo[-g]
        halo[g] += halo[-g]

    returns = []
    for g, (ex, dxs) in enumerate(groups):
        for copy in halo[g]:
            copy.wait_recv()
        for first, dx in enumerate(dxs):
            tiles = tiles_of(dx)
            C = crecv[g, 1]
            CG = jnp.where(
                row_y == Y - 1, pltpu.roll(crecv[g, 2], Y - 1, 0), pltpu.roll(crecv[g, 0], 8 - (Y - 1), 0)
            )
            for c in range(6):
                Gy[c, pl.ds(Y - 1, slots, stride=Y), :] = yrecv[g, 1, c]
                Gy[c, pl.ds(0, slots, stride=Y), :] = yrecv[g, 0, c]

            def zshift(x, col, c):
                edge = jnp.concatenate(
                    [pltpu.roll(col, Z - 1 - (c * nv + v), 1) for v in range(nv)], axis=0
                )
                return jnp.where(lane_f == Z - 1, edge, pltpu.roll(x, Z - 1, 1))

            for c in range(6):
                x0, g0 = V[g, c], Gy[c]
                x1, g1 = zshift(x0, C, c), zshift(g0, CG, c)
                for j, (k, d) in enumerate(tiles):
                    x, gh = (x1, g1) if d[2] else (x0, g0)
                    if d[1] == 1:
                        x = jnp.where(rowy_f == Y - 1, gh, pltpu.roll(x, rows - 1, 0))
                    elif d[1] == -1:
                        x = jnp.where(rowy_f == 0, gh, pltpu.roll(x, 1, 0))
                    if c < 3 and d[c]:
                        x = x + float(d[c])
                    oth[j, c] = x

            k0, step = tiles[0][0], tiles[1][0] - tiles[0][0]

            def tile_loop(i, carry, k0=k0, step=step):
                j = i // (rows // 16)
                h = i - j * (rows // 16)
                k = k0 + step * j

                def theta_of(s, base):
                    return nz[k, s, pl.ds(base, 16), :].astype(jnp.float32)

                pair_rows(j, h, theta_of, False)
                return carry

            lax.fori_loop(0, len(tiles) * (rows // 16), tile_loop, 0)

            RC = jnp.zeros((8, Z), jnp.float32)
            RCG = jnp.zeros((8, Z), jnp.float32)
            for b in range(3):
                loc, gho = [0.0, 0.0], [0.0, 0.0]
                for j, (k, d) in enumerate(tiles):
                    x = Bs[j, b]
                    z = d[2]
                    if d[1] == 0:
                        loc[z] = loc[z] + x
                    elif d[1] == 1:
                        loc[z] = loc[z] + jnp.where(rowy_f == 0, 0.0, pltpu.roll(x, 1, 0))
                        gho[z] = gho[z] + jnp.where(rowy_f == Y - 1, x, 0.0)
                    else:
                        loc[z] = loc[z] + jnp.where(rowy_f == Y - 1, 0.0, pltpu.roll(x, rows - 1, 0))
                        gho[z] = gho[z] + jnp.where(rowy_f == 0, x, 0.0)
                lz, gz = pltpu.roll(loc[1], 1, 1), pltpu.roll(gho[1], 1, 1)
                total = loc[0] + jnp.where(lane_f == 0, 0.0, lz)
                gtotal = gho[0] + jnp.where(lane_f == 0, 0.0, gz)
                if first:
                    total = total + R[g, b]
                    gtotal = gtotal + Gacc[b]
                R[g, b] = total
                Gacc[b] = gtotal
                for v in range(nv):
                    i = b * nv + v
                    xl, xg = lz[v * 8 : v * 8 + 8], gz[v * 8 : v * 8 + 8]
                    RC = jnp.where(lane == i, pltpu.roll(xl, i, 1) if i else xl, RC)
                    RCG = jnp.where(lane == i, pltpu.roll(xg, i, 1) if i else xg, RCG)
            if first:
                RC = RC + RCsend[g, 0]
                RCG = RCG + RCsend[g, 1]
            RCsend[g, 0] = RC
            RCsend[g, 1] = RCG
        for b in range(3):
            RGsend[g, 1, b] = Gacc[b, pl.ds(Y - 1, slots, stride=Y), :]
            RGsend[g, 0, b] = Gacc[b, pl.ds(0, slots, stride=Y), :]
        if g:
            returns.append(send(R.at[g], Rrecv.at[g], (ex, 0, 0)))
        returns.append(send(RGsend.at[g, 1], RGrecv.at[g, 1], (ex, 1, 0)))
        returns.append(send(RGsend.at[g, 0], RGrecv.at[g, 0], (ex, -1, 0)))
        for e in (-1, 0, 1):
            returns.append(send(RCsend.at[g, 0 if e == 0 else 1], RCrecv.at[g, e + 1], (ex, e, 1)))

    for q, (a, b) in enumerate(PAIRS):
        total = vacc[q]
        for s in range(slots):
            total = total + own[s, a] * accA[s, b]
        stat[pl.ds(q, 1), :] = jnp.sum(total, axis=0, keepdims=True)
    here = me[0] * ny + me[1]
    sums = []
    for ex in range(nx):
        for ey in range(ny):
            if (ex, ey) != (0, 0):
                sums.append(send(stat, statxy.at[here], (ex, ey, 0)))
    statxy[here] = stat[...]

    for b in range(3):
        packed = []
        for v in range(nv):
            out = None
            for u in range(G):
                x = accA[v * G + u, b]
                y = x
                for r in range(1, G):
                    y = y + pltpu.roll(x, r * Y, 0)
                out = y if out is None else jnp.where(row // Y == u, y, out)
            packed.append(out)
        R[0, b] = jnp.concatenate(packed, axis=0) - R[0, b]

    for copy in sums:
        copy.wait_recv()
    plane = statxy[0]
    for i in range(1, nx * ny):
        plane = plane + statxy[i]
    statp[...] = plane
    last = []
    for ez in range(1, nz_dev):
        last.append(send(statp, statz.at[me[2]], (0, 0, ez)))
    statz[me[2]] = plane

    for copy in returns:
        copy.wait_recv()
    corner = jnp.zeros((8, Z), jnp.float32)
    for g in range(ng):
        corner = corner + RCrecv[g, 1]
        corner = corner + jnp.where(row_y == 0, pltpu.roll(RCrecv[g, 0 + 2], 8 - (Y - 1), 0), 0.0)
        corner = corner + jnp.where(row_y == Y - 1, pltpu.roll(RCrecv[g, 0], Y - 1, 0), 0.0)
    for b in range(3):
        low = RGrecv[0, 1, b]
        high = RGrecv[0, 0, b]
        for g in range(1, ng):
            low = low + RGrecv[g, 1, b]
            high = high + RGrecv[g, 0, b]
        R[0, b, pl.ds(0, slots, stride=Y), :] = R[0, b, pl.ds(0, slots, stride=Y), :] - low
        R[0, b, pl.ds(Y - 1, slots, stride=Y), :] = R[0, b, pl.ds(Y - 1, slots, stride=Y), :] - high
        edge = jnp.concatenate(
            [pltpu.roll(corner, (Z - (b * nv + v)) % Z, 1) if b + v else corner for v in range(nv)], axis=0
        )
        total = R[0, b] - jnp.where(lane_f == 0, edge, 0.0)
        for g in range(1, ng):
            total = total - Rrecv[g, b]
        push_ref[b] = total

    for copy in last:
        copy.wait_recv()
    total = statz[0]
    for i in range(1, nz_dev):
        total = total + statz[i]
    total = jnp.sum(total, axis=1, keepdims=True)
    volume = Y * Z * nx * ny * nz_dev
    r3 = lax.broadcasted_iota(jnp.int32, (3, 3), 0)
    c3 = lax.broadcasted_iota(jnp.int32, (3, 3), 1)
    stress = jnp.zeros((3, 3), jnp.float32)
    for q, (a, b) in enumerate(PAIRS):
        hit = ((r3 == a) & (c3 == b)) | ((r3 == b) & (c3 == a))
        val = jnp.broadcast_to(total[6 + q : 7 + q] + total[q : q + 1], (3, 3))
        stress = jnp.where(hit, val, stress)
    stress_ref[...] = stress / volume
    thermal_ref[...] = (total[6:7] + total[9:10] + total[11:12]) / (3.0 * total[12:13] - 3.0)
    for copy in every + returns + sums + last:
        copy.wait_send()


def per_device(sizes, offset, velocity, occupancy, noise):
    slots, size_x, Y, Z = offset.shape[1:]
    assert size_x == 1 and slots == 8 and 8 % Y == 0 and Y > 1 and (slots * Y) % 16 == 0
    nx, ny, nzd = sizes
    rows = slots * Y
    ng = len(groups_of(nx))
    f32 = jnp.float32
    copies = (ng * 5 + ng - 1) * 2 + nx * ny - 1 + nzd - 1
    vm = lambda *shape: pltpu.VMEM(shape, f32)
    spec = pl.BlockSpec(memory_space=pltpu.VMEM)
    push, stress, thermal = pl.pallas_call(
        functools.partial(kernel, sizes, slots, Y),
        out_shape=(
            jax.ShapeDtypeStruct((3, rows, Z), f32),
            jax.ShapeDtypeStruct((3, 3), f32),
            jax.ShapeDtypeStruct((1, 1), f32),
        ),
        in_specs=[spec, spec, spec, pl.BlockSpec(memory_space=pl.ANY)],
        out_specs=(spec, spec, spec),
        scratch_shapes=[
            pltpu.VMEM((14, slots, rows, Z), jnp.bfloat16),
            vm(slots, rows, Z),
            vm(slots, 6, 8, Z),
            vm(ng, 6, rows, Z),
            vm(2, 6, slots, Z),
            vm(ng, 2, 6, slots, Z),
            vm(6, rows, Z),
            vm(8, Z),
            vm(ng, 3, 8, Z),
            vm(5, 6, rows, Z),
            vm(5, 3, rows, Z),
            vm(slots, 3, 8, Z),
            vm(6, 8, Z),
            vm(ng, 3, rows, Z),
            vm(ng, 3, rows, Z),
            vm(3, rows, Z),
            vm(ng, 2, 3, slots, Z),
            vm(ng, 2, 3, slots, Z),
            vm(ng, 2, 8, Z),
            vm(ng, 3, 8, Z),
            vm(16, Z),
            vm(nx * ny, 16, Z),
            vm(16, Z),
            vm(nzd, 16, Z),
            pltpu.SemaphoreType.DMA,
            pltpu.SemaphoreType.DMA((copies,)),
            pltpu.SemaphoreType.DMA((copies,)),
        ],
        compiler_params=pltpu.CompilerParams(collective_id=0, has_side_effects=True),
    )(
        offset.reshape(3, rows, Z),
        velocity.reshape(3, rows, Z),
        occupancy.reshape(Y, Z),
        noise.reshape(14, slots, rows, Z),
    )
    return push.reshape(offset.shape), stress, thermal.reshape(1)


def solution(mesh):
    placed = (
        P(None, None, "gx", "gy", "gz"),
        P(None, None, "gx", "gy", "gz"),
        P("gx", "gy", "gz"),
        P(None, None, None, "gx", "gy", "gz"),
    )
    sizes = tuple(mesh.shape[a] for a in ("gx", "gy", "gz"))
    return jax.shard_map(
        functools.partial(per_device, sizes),
        mesh=mesh,
        in_specs=placed,
        out_specs=(P(None, None, "gx", "gy", "gz"), P(), P()),
        check_vma=False,
    )
```

```python
import functools
import jax
import jax.numpy as jnp
from jax import lax
from jax.experimental import pallas as pl
from jax.experimental.pallas import tpu as pltpu
from jax.sharding import PartitionSpec as P

REPULSION = 25.0
FRICTION = 4.5
NOISE_SCALE = 15.0
FAR = 64.0
PAIRS = ((0, 0), (0, 1), (0, 2), (1, 1), (1, 2), (2, 2))
forward_shifts = [(1, 0, 0), (-1, 1, 0), (0, 1, 0), (1, 1, 0)] + [
    (dx, dy, 1) for dy in (-1, 0, 1) for dx in (-1, 0, 1)
]
MESH = pl.DeviceIdType.MESH


def tiles_of(dx):
    return [(k + 1, d) for k, d in enumerate(forward_shifts) if d[0] == dx]


def groups_of(nx):
    if nx == 2:
        return [(0, (0,)), (1, (1, -1))]
    return [(0, (0,)), (1, (1,)), (-1, (-1,))]


def phases_of(sizes):
    nx, ny, nz_dev = sizes
    plane = [(ex, ey, 0) for ex in range(nx) for ey in range(ny)]
    if nx * ny * nz_dev <= 64:
        return [[(ex, ey, ez) for ez in range(nz_dev) for ex, ey, _ in plane]]
    return [plane, [(0, 0, ez) for ez in range(nz_dev)]]


def finish(push_in, stress_in, thermal_in, push, stress, thermal):
    push[...] = push_in[...]
    stress[...] = stress_in[...]
    thermal[...] = thermal_in[...]


def kernel(
    sizes, slots, Y,
    off_hbm, vel_hbm, occ_hbm, noise_ref,
    push_ref, stress_ref, thermal_ref,
    off_ref, vel_ref, occ_ref, nz, n0, own, V, ysend, yrecv, Gy, csend, crecv, oth, Bs, accA, vacc,
    R, Rrecv, Gacc, RGsend, RGrecv, RCsend, RCrecv, stat, row_send, row_recv, plane_send, plane_recv,
    nsem, ssem, rsem,
):
    nx, ny, nz_dev = sizes
    rows = slots * Y
    Z = off_ref.shape[2]
    G = 8 // Y
    nv = rows // 8
    groups = groups_of(nx)
    ng = len(groups)
    me = (lax.axis_index("gx"), lax.axis_index("gy"), lax.axis_index("gz"))

    def dev(e):
        return tuple(lax.rem(m + (o % n), n) for m, o, n in zip(me, e, sizes))

    partners = set()
    for ex, _ in groups:
        for ey in (-1, 0, 1):
            for ez in (-1, 0, 1):
                partners.add((ex % nx, ey % ny, ez % nz_dev))
                partners.add((-ex % nx, ey % ny, ez % nz_dev))
    phases = phases_of(sizes)
    for phase in phases:
        partners.update(phase)
    partners.discard((0, 0, 0))
    partners = sorted(partners)
    barrier = pltpu.get_barrier_semaphore()
    for e in partners:
        pl.semaphore_signal(barrier, inc=1, device_id=dev(e), device_id_type=MESH)

    loads = [
        pltpu.make_async_copy(off_hbm, off_ref, nsem.at[0]),
        pltpu.make_async_copy(vel_hbm, vel_ref, nsem.at[1]),
        pltpu.make_async_copy(occ_hbm, occ_ref, nsem.at[2]),
        pltpu.make_async_copy(noise_ref.at[0], nz.at[0], nsem.at[3]),
        pltpu.make_async_copy(noise_ref.at[pl.ds(1, 13)], nz.at[pl.ds(1, 13)], nsem.at[4]),
    ]
    for load in loads:
        load.start()

    lane = lax.broadcasted_iota(jnp.int32, (8, Z), 1)
    row = lax.broadcasted_iota(jnp.int32, (8, Z), 0)
    row_y = lax.rem(row, Y)
    lane_f = lax.broadcasted_iota(jnp.int32, (rows, Z), 1)
    row_f = lax.broadcasted_iota(jnp.int32, (rows, Z), 0)
    rowy_f = lax.rem(row_f, Y)
    slot_f = row_f // Y

    for load in loads[:3]:
        load.wait()
    occ = occ_ref[...]
    occ8 = jnp.concatenate([occ] * G, axis=0)
    occ_f = jnp.concatenate([occ8] * nv, axis=0)
    live_f = slot_f < occ_f
    for c in range(3):
        x = off_ref[c]
        if c == 0:
            V[0, 0] = jnp.where(live_f, x, FAR)
        else:
            V[0, c] = x
        V[0, 3 + c] = vel_ref[c] * FRICTION
    for s in range(slots):
        for c in range(3):
            x = off_ref[c, pl.ds(s * Y, Y), :]
            x = jnp.concatenate([x] * G, axis=0)
            if c == 0:
                x = jnp.where(occ8 > s, x, -FAR)
            own[s, c] = x
            v = vel_ref[c, pl.ds(s * Y, Y), :] * FRICTION
            own[s, 3 + c] = jnp.concatenate([v] * G, axis=0)
    compact = jnp.zeros((8, Z), jnp.float32)
    for c in range(6):
        ysend[0, c] = V[0, c, pl.ds(Y - 1, slots, stride=Y), :]
        ysend[1, c] = V[0, c, pl.ds(0, slots, stride=Y), :]
        for v in range(nv):
            i = c * nv + v
            x = V[0, c, pl.ds(v * 8, 8), :]
            compact = jnp.where(lane == i, pltpu.roll(x, i, 1) if i else x, compact)
    csend[...] = compact

    def fold(x):
        total = x[0:8]
        for v in range(1, nv):
            total = total + x[v * 8 : v * 8 + 8]
        return total

    vels = [jnp.where(live_f, vel_ref[c], 0.0) for c in range(3)]
    lines = [jnp.sum(fold(vels[a] * vels[b]), axis=0, keepdims=True) for a, b in PAIRS]
    lines.append(jnp.sum(fold(live_f.astype(jnp.float32)), axis=0, keepdims=True))
    lines.append(jnp.zeros((1, Z), jnp.float32))
    stat[pl.ds(8, 8), :] = jnp.concatenate(lines, axis=0)
    accA[...] = jnp.zeros(accA.shape, jnp.float32)
    vacc[...] = jnp.zeros(vacc.shape, jnp.float32)

    def pair_rows(j, h, theta_of, self_tile):
        base = pl.multiple_of(h * 16, 16)
        src = V if self_tile else oth
        other = [src[j, c, pl.ds(base, 16), :].reshape(2, 8, Z) for c in range(6)]
        B = [jnp.zeros((2, 8, Z), jnp.float32) for _ in range(3)]
        for s in range(slots):
            theta = theta_of(s, base).reshape(2, 8, Z)
            mine = [own[s, c] for c in range(6)]
            sep = [mine[c][None] - other[c] for c in range(3)]
            rel = [mine[3 + c][None] - other[3 + c] for c in range(3)]
            dist2 = sep[0] * sep[0] + sep[1] * sep[1] + sep[2] * sep[2]
            if self_tile:
                pos = lax.broadcasted_iota(jnp.int32, (2, 8, Z), 0) * 8
                pos = pos + lax.broadcasted_iota(jnp.int32, (2, 8, Z), 1) + h * 16
                dist2 = jnp.where(pos // Y == s, 4.0, dist2)
            inv = lax.rsqrt(dist2)
            w = jnp.maximum(1.0 - dist2 * inv, 0.0)
            closing = (sep[0] * rel[0] + sep[1] * rel[1] + sep[2] * rel[2]) * inv
            f = w * (REPULSION + NOISE_SCALE * theta - w * closing) * inv
            for c in range(3):
                F = f * sep[c]
                if not self_tile:
                    B[c] = B[c] + F
                accA[s, c] = accA[s, c] + (F[0] + F[1])
        if not self_tile:
            for c in range(3):
                Bs[j, c, pl.ds(base, 16), :] = B[c].reshape(16, Z)
            for q, (a, b) in enumerate(PAIRS):
                m = other[a] * B[b]
                vacc[q] = vacc[q] - (m[0] + m[1])

    loads[3].wait()
    for t in range(slots):
        x = nz[0, t].astype(jnp.float32)
        for s in range(slots):
            n0[s, pl.ds(t * Y, Y), :] = x[s * Y : s * Y + Y]

    def self_loop(h, carry):
        def theta_of(s, base):
            straight = nz[0, s, pl.ds(base, 16), :].astype(jnp.float32)
            return (straight + n0[s, pl.ds(base, 16), :]) * 0.7071067811865476

        pair_rows(0, h, theta_of, True)
        return carry

    lax.fori_loop(0, rows // 16, self_loop, 0)

    pl.semaphore_wait(barrier, len(partners))

    count = [0]

    def send(src, dst, e):
        i = count[0]
        count[0] += 1
        copy = pltpu.make_async_remote_copy(
            src_ref=src, dst_ref=dst, send_sem=ssem.at[i], recv_sem=rsem.at[i],
            device_id=dev(e), device_id_type=MESH,
        )
        copy.start()
        return copy

    halo = {g: [] for g in range(ng)}
    for g, (ex, _) in enumerate(groups):
        for e in (0, 1, -1):
            halo[g].append(send(csend, crecv.at[g, e + 1], (-ex, -e, -1)))
    for g, (ex, _) in enumerate(groups):
        if g:
            halo[g].append(send(V.at[0], V.at[g], (-ex, 0, 0)))
    for g, (ex, _) in enumerate(groups):
        halo[g].append(send(ysend.at[1], yrecv.at[g, 1], (-ex, -1, 0)))
        halo[g].append(send(ysend.at[0], yrecv.at[g, 0], (-ex, 1, 0)))
    every = [copy for g in range(ng) for copy in halo[g]]
    loads[4].wait()

    def send_sums():
        lines = []
        for q, (a, b) in enumerate(PAIRS):
            total = vacc[q]
            for s in range(slots):
                total = total + own[s, a] * accA[s, b]
            lines.append(jnp.sum(total, axis=0, keepdims=True))
        lines.append(jnp.zeros((2, Z), jnp.float32))
        stat[pl.ds(0, 8), :] = jnp.concatenate(lines, axis=0)
        column = jnp.sum(stat[...], axis=1, keepdims=True)
        r16 = lax.broadcasted_iota(jnp.int32, (16, Z), 0)
        l16 = lax.broadcasted_iota(jnp.int32, (16, Z), 1)
        line = jnp.sum(jnp.where(r16 == l16, jnp.broadcast_to(column, (16, Z)), 0.0), axis=0, keepdims=True)
        row_send[...] = jnp.broadcast_to(line, (8, Z))
        row_recv[here] = jnp.broadcast_to(line, (8, Z))
        return [
            send(row_send.at[pl.ds(0, 1)], row_recv.at[here, pl.ds(0, 1)], e) for e in phases[0] if e != (0, 0, 0)
        ]

    one_phase = len(phases) == 1
    here = me[0] * ny + me[1]
    if one_phase:
        here = here * nz_dev + me[2]
    returns = []
    for g, (ex, dxs) in enumerate(groups):
        for copy in halo[g]:
            copy.wait_recv()
        for first, dx in enumerate(dxs):
            tiles = tiles_of(dx)
            C = crecv[g, 1]
            CG = jnp.where(
                row_y == Y - 1, pltpu.roll(crecv[g, 2], Y - 1, 0), pltpu.roll(crecv[g, 0], 8 - (Y - 1), 0)
            )
            for c in range(6):
                Gy[c, pl.ds(Y - 1, slots, stride=Y), :] = yrecv[g, 1, c]
                Gy[c, pl.ds(0, slots, stride=Y), :] = yrecv[g, 0, c]

            def zshift(x, col, c):
                edge = jnp.concatenate(
                    [pltpu.roll(col, Z - 1 - (c * nv + v), 1) for v in range(nv)], axis=0
                )
                return jnp.where(lane_f == Z - 1, edge, pltpu.roll(x, Z - 1, 1))

            for c in range(6):
                x0, g0 = V[g, c], Gy[c]
                x1, g1 = zshift(x0, C, c), zshift(g0, CG, c)
                for j, (k, d) in enumerate(tiles):
                    x, gh = (x1, g1) if d[2] else (x0, g0)
                    if d[1] == 1:
                        x = jnp.where(rowy_f == Y - 1, gh, pltpu.roll(x, rows - 1, 0))
                    elif d[1] == -1:
                        x = jnp.where(rowy_f == 0, gh, pltpu.roll(x, 1, 0))
                    if c < 3 and d[c]:
                        x = x + float(d[c])
                    oth[j, c] = x

            k0, step = tiles[0][0], tiles[1][0] - tiles[0][0]

            def tile_loop(i, carry, k0=k0, step=step):
                j = i // (rows // 16)
                h = i - j * (rows // 16)
                k = k0 + step * j

                def theta_of(s, base):
                    return nz[k, s, pl.ds(base, 16), :].astype(jnp.float32)

                pair_rows(j, h, theta_of, False)
                return carry

            lax.fori_loop(0, len(tiles) * (rows // 16), tile_loop, 0)

            if g == ng - 1 and dx == dxs[-1]:
                sums = send_sums()

            RC = jnp.zeros((8, Z), jnp.float32)
            RCG = jnp.zeros((8, Z), jnp.float32)
            for b in range(3):
                loc, gho = [0.0, 0.0], [0.0, 0.0]
                for j, (k, d) in enumerate(tiles):
                    x = Bs[j, b]
                    z = d[2]
                    if d[1] == 0:
                        loc[z] = loc[z] + x
                    elif d[1] == 1:
                        loc[z] = loc[z] + jnp.where(rowy_f == 0, 0.0, pltpu.roll(x, 1, 0))
                        gho[z] = gho[z] + jnp.where(rowy_f == Y - 1, x, 0.0)
                    else:
                        loc[z] = loc[z] + jnp.where(rowy_f == Y - 1, 0.0, pltpu.roll(x, rows - 1, 0))
                        gho[z] = gho[z] + jnp.where(rowy_f == 0, x, 0.0)
                lz, gz = pltpu.roll(loc[1], 1, 1), pltpu.roll(gho[1], 1, 1)
                total = loc[0] + jnp.where(lane_f == 0, 0.0, lz)
                gtotal = gho[0] + jnp.where(lane_f == 0, 0.0, gz)
                if first:
                    total = total + R[g, b]
                    gtotal = gtotal + Gacc[b]
                R[g, b] = total
                Gacc[b] = gtotal
                for v in range(nv):
                    i = b * nv + v
                    xl, xg = lz[v * 8 : v * 8 + 8], gz[v * 8 : v * 8 + 8]
                    RC = jnp.where(lane == i, pltpu.roll(xl, i, 1) if i else xl, RC)
                    RCG = jnp.where(lane == i, pltpu.roll(xg, i, 1) if i else xg, RCG)
            if first:
                RC = RC + RCsend[g, 0]
                RCG = RCG + RCsend[g, 1]
            RCsend[g, 0] = RC
            RCsend[g, 1] = RCG
        for b in range(3):
            RGsend[g, 1, b] = Gacc[b, pl.ds(Y - 1, slots, stride=Y), :]
            RGsend[g, 0, b] = Gacc[b, pl.ds(0, slots, stride=Y), :]
        if g:
            returns.append(send(R.at[g], Rrecv.at[g], (ex, 0, 0)))
        returns.append(send(RGsend.at[g, 1], RGrecv.at[g, 1], (ex, 1, 0)))
        returns.append(send(RGsend.at[g, 0], RGrecv.at[g, 0], (ex, -1, 0)))
        for e in (-1, 0, 1):
            returns.append(send(RCsend.at[g, 0 if e == 0 else 1], RCrecv.at[g, e + 1], (ex, e, 1)))

    for b in range(3):
        packed = []
        for v in range(nv):
            out = None
            for u in range(G):
                x = accA[v * G + u, b]
                y = x
                for r in range(1, G):
                    y = y + pltpu.roll(x, r * Y, 0)
                out = y if out is None else jnp.where(row // Y == u, y, out)
            packed.append(out)
        R[0, b] = jnp.concatenate(packed, axis=0) - R[0, b]

    last = []
    if not one_phase:
        for copy in sums:
            copy.wait_recv()
        plane = row_recv[0]
        for i in range(1, nx * ny):
            plane = plane + row_recv[i]
        plane_send[...] = plane
        plane_recv[me[2]] = plane
        for e in phases[1]:
            if e != (0, 0, 0):
                last.append(send(plane_send, plane_recv.at[me[2]], e))

    for copy in returns:
        copy.wait_recv()
    corner = jnp.zeros((8, Z), jnp.float32)
    for g in range(ng):
        corner = corner + RCrecv[g, 1]
        corner = corner + jnp.where(row_y == 0, pltpu.roll(RCrecv[g, 0 + 2], 8 - (Y - 1), 0), 0.0)
        corner = corner + jnp.where(row_y == Y - 1, pltpu.roll(RCrecv[g, 0], Y - 1, 0), 0.0)
    for b in range(3):
        low = RGrecv[0, 1, b]
        high = RGrecv[0, 0, b]
        for g in range(1, ng):
            low = low + RGrecv[g, 1, b]
            high = high + RGrecv[g, 0, b]
        R[0, b, pl.ds(0, slots, stride=Y), :] = R[0, b, pl.ds(0, slots, stride=Y), :] - low
        R[0, b, pl.ds(Y - 1, slots, stride=Y), :] = R[0, b, pl.ds(Y - 1, slots, stride=Y), :] - high
        edge = jnp.concatenate(
            [pltpu.roll(corner, (Z - (b * nv + v)) % Z, 1) if b + v else corner for v in range(nv)], axis=0
        )
        total = R[0, b] - jnp.where(lane_f == 0, edge, 0.0)
        for g in range(1, ng):
            total = total - Rrecv[g, b]
        push_ref[b] = total

    for copy in sums if one_phase else last:
        copy.wait_recv()
    source, parts = (row_recv, nx * ny * nz_dev) if one_phase else (plane_recv, nz_dev)
    terms = [source[i, pl.ds(0, 1), :] for i in range(parts)]
    while len(terms) > 1:
        odd = terms[len(terms) // 2 * 2 :]
        terms = [terms[i] + terms[i + 1] for i in range(0, len(terms) - 1, 2)] + odd
    total = terms[0]
    item = lambda i: total[:, i : i + 1]
    volume = Y * Z * nx * ny * nz_dev
    r3 = lax.broadcasted_iota(jnp.int32, (3, 3), 0)
    c3 = lax.broadcasted_iota(jnp.int32, (3, 3), 1)
    stress = jnp.zeros((3, 3), jnp.float32)
    for q, (a, b) in enumerate(PAIRS):
        hit = ((r3 == a) & (c3 == b)) | ((r3 == b) & (c3 == a))
        val = jnp.broadcast_to(item(8 + q) + item(q), (3, 3))
        stress = jnp.where(hit, val, stress)
    stress_ref[...] = stress / volume
    thermal_ref[...] = (item(8) + item(11) + item(13)) / (3.0 * item(14) - 3.0)
    for copy in every + returns + sums + last:
        copy.wait_send()


def per_device(sizes, offset, velocity, occupancy, noise):
    slots, size_x, Y, Z = offset.shape[1:]
    assert size_x == 1 and slots == 8 and 8 % Y == 0 and Y > 1 and (slots * Y) % 16 == 0
    nx, ny, nzd = sizes
    rows = slots * Y
    ng = len(groups_of(nx))
    f32 = jnp.float32
    phases = phases_of(sizes)
    copies = (ng * 5 + ng - 1) * 2 + sum(len(phase) - 1 for phase in phases)
    vm = lambda *shape: pltpu.VMEM(shape, f32)
    spec = pl.BlockSpec(memory_space=pltpu.VMEM)
    outs = (
        jax.ShapeDtypeStruct((3, rows, Z), f32),
        jax.ShapeDtypeStruct((3, 3), f32),
        jax.ShapeDtypeStruct((1, 1), f32),
    )
    results = pl.pallas_call(
        functools.partial(kernel, sizes, slots, Y),
        out_shape=outs,
        in_specs=[pl.BlockSpec(memory_space=pl.ANY)] * 4,
        out_specs=(spec, spec, spec),
        scratch_shapes=[
            vm(3, rows, Z),
            vm(3, rows, Z),
            pltpu.VMEM((Y, Z), jnp.int32),
            pltpu.VMEM((14, slots, rows, Z), jnp.bfloat16),
            vm(slots, rows, Z),
            vm(slots, 6, 8, Z),
            vm(ng, 6, rows, Z),
            vm(2, 6, slots, Z),
            vm(ng, 2, 6, slots, Z),
            vm(6, rows, Z),
            vm(8, Z),
            vm(ng, 3, 8, Z),
            vm(5, 6, rows, Z),
            vm(5, 3, rows, Z),
            vm(slots, 3, 8, Z),
            vm(6, 8, Z),
            vm(ng, 3, rows, Z),
            vm(ng, 3, rows, Z),
            vm(3, rows, Z),
            vm(ng, 2, 3, slots, Z),
            vm(ng, 2, 3, slots, Z),
            vm(ng, 2, 8, Z),
            vm(ng, 3, 8, Z),
            vm(16, Z),
            vm(8, Z),
            vm(len(phases[0]), 8, Z),
            vm(8, Z),
            vm(nzd, 8, Z),
            pltpu.SemaphoreType.DMA((5,)),
            pltpu.SemaphoreType.DMA((copies,)),
            pltpu.SemaphoreType.DMA((copies,)),
        ],
        compiler_params=pltpu.CompilerParams(collective_id=0, has_side_effects=True),
    )(
        offset.reshape(3, rows, Z),
        velocity.reshape(3, rows, Z),
        occupancy.reshape(Y, Z),
        noise.reshape(14, slots, rows, Z),
    )
    push, stress, thermal = pl.pallas_call(
        finish, out_shape=outs, in_specs=[spec] * 3, out_specs=(spec, spec, spec)
    )(*results)
    return push.reshape(offset.shape), stress, thermal.reshape(1)


def solution(mesh):
    placed = (
        P(None, None, "gx", "gy", "gz"),
        P(None, None, "gx", "gy", "gz"),
        P("gx", "gy", "gz"),
        P(None, None, None, "gx", "gy", "gz"),
    )
    sizes = tuple(mesh.shape[a] for a in ("gx", "gy", "gz"))
    return jax.shard_map(
        functools.partial(per_device, sizes),
        mesh=mesh,
        in_specs=placed,
        out_specs=(P(None, None, "gx", "gy", "gz"), P(), P()),
        check_vma=False,
    )
```

```python
import functools
import jax
import jax.numpy as jnp
from jax import lax
from jax.experimental import pallas as pl
from jax.experimental.pallas import tpu as pltpu
from jax.sharding import PartitionSpec as P

REPULSION = 25.0
FRICTION = 4.5
NOISE_SCALE = 15.0
FAR = 64.0
PAIRS = ((0, 0), (0, 1), (0, 2), (1, 1), (1, 2), (2, 2))
forward_shifts = [(1, 0, 0), (-1, 1, 0), (0, 1, 0), (1, 1, 0)] + [
    (dx, dy, 1) for dy in (-1, 0, 1) for dx in (-1, 0, 1)
]
MESH = pl.DeviceIdType.MESH


def tiles_of(dx):
    return [(k + 1, d) for k, d in enumerate(forward_shifts) if d[0] == dx]


def groups_of(nx):
    if nx == 2:
        return [(0, (0,)), (1, (1, -1))]
    return [(0, (0,)), (1, (1,)), (-1, (-1,))]


def phases_of(sizes):
    nx, ny, nz_dev = sizes
    plane = [(ex, ey, 0) for ex in range(nx) for ey in range(ny)]
    if nx * ny * nz_dev <= 64:
        return [[(ex, ey, ez) for ez in range(nz_dev) for ex, ey, _ in plane]]
    return [plane, [(0, 0, ez) for ez in range(nz_dev)]]


def finish(volume, push_in, total_in, push, stress, thermal):
    push[...] = push_in[...]
    total = total_in[0:1, :]
    item = lambda i: total[:, i : i + 1]
    r3 = lax.broadcasted_iota(jnp.int32, (3, 3), 0)
    c3 = lax.broadcasted_iota(jnp.int32, (3, 3), 1)
    matrix = jnp.zeros((3, 3), jnp.float32)
    for q, (a, b) in enumerate(PAIRS):
        hit = ((r3 == a) & (c3 == b)) | ((r3 == b) & (c3 == a))
        val = jnp.broadcast_to(item(8 + q) + item(q), (3, 3))
        matrix = jnp.where(hit, val, matrix)
    stress[...] = matrix / volume
    thermal[...] = (item(8) + item(11) + item(13)) / (3.0 * item(14) - 3.0)


def kernel(
    sizes, slots, Y,
    off_hbm, vel_hbm, occ_hbm, noise_ref,
    push_ref, total_ref,
    off_ref, vel_ref, occ_ref, nz, n0, own, V, ysend, yrecv, Gy, csend, crecv, oth, Bs, accA, vacc,
    R, Rrecv, Gacc, RGsend, RGrecv, RCsend, RCrecv, stat, row_send, row_recv, plane_send, plane_recv,
    nsem, ssem, rsem,
):
    nx, ny, nz_dev = sizes
    rows = slots * Y
    Z = off_ref.shape[2]
    G = 8 // Y
    nv = rows // 8
    groups = groups_of(nx)
    ng = len(groups)
    me = (lax.axis_index("gx"), lax.axis_index("gy"), lax.axis_index("gz"))

    def dev(e):
        return tuple(lax.rem(m + (o % n), n) for m, o, n in zip(me, e, sizes))

    partners = set()
    for ex, _ in groups:
        for ey in (-1, 0, 1):
            for ez in (-1, 0, 1):
                partners.add((ex % nx, ey % ny, ez % nz_dev))
                partners.add((-ex % nx, ey % ny, ez % nz_dev))
    phases = phases_of(sizes)
    for phase in phases:
        partners.update(phase)
    partners.discard((0, 0, 0))
    partners = sorted(partners)
    barrier = pltpu.get_barrier_semaphore()
    for e in partners:
        pl.semaphore_signal(barrier, inc=1, device_id=dev(e), device_id_type=MESH)

    loads = [
        pltpu.make_async_copy(off_hbm, off_ref, nsem.at[0]),
        pltpu.make_async_copy(vel_hbm, vel_ref, nsem.at[1]),
        pltpu.make_async_copy(occ_hbm, occ_ref, nsem.at[2]),
        pltpu.make_async_copy(noise_ref.at[0], nz.at[0], nsem.at[3]),
        pltpu.make_async_copy(noise_ref.at[pl.ds(1, 13)], nz.at[pl.ds(1, 13)], nsem.at[4]),
    ]
    for load in loads:
        load.start()

    lane = lax.broadcasted_iota(jnp.int32, (8, Z), 1)
    row = lax.broadcasted_iota(jnp.int32, (8, Z), 0)
    row_y = lax.rem(row, Y)
    lane_f = lax.broadcasted_iota(jnp.int32, (rows, Z), 1)
    row_f = lax.broadcasted_iota(jnp.int32, (rows, Z), 0)
    rowy_f = lax.rem(row_f, Y)
    slot_f = row_f // Y

    for load in loads[:3]:
        load.wait()
    occ = occ_ref[...]
    occ8 = jnp.concatenate([occ] * G, axis=0)
    occ_f = jnp.concatenate([occ8] * nv, axis=0)
    live_f = slot_f < occ_f
    for c in range(3):
        x = off_ref[c]
        if c == 0:
            V[0, 0] = jnp.where(live_f, x, FAR)
        else:
            V[0, c] = x
        V[0, 3 + c] = vel_ref[c] * FRICTION
    for s in range(slots):
        for c in range(3):
            x = off_ref[c, pl.ds(s * Y, Y), :]
            x = jnp.concatenate([x] * G, axis=0)
            if c == 0:
                x = jnp.where(occ8 > s, x, -FAR)
            own[s, c] = x
            v = vel_ref[c, pl.ds(s * Y, Y), :] * FRICTION
            own[s, 3 + c] = jnp.concatenate([v] * G, axis=0)
    compact = jnp.zeros((8, Z), jnp.float32)
    for c in range(6):
        ysend[0, c] = V[0, c, pl.ds(Y - 1, slots, stride=Y), :]
        ysend[1, c] = V[0, c, pl.ds(0, slots, stride=Y), :]
        for v in range(nv):
            i = c * nv + v
            x = V[0, c, pl.ds(v * 8, 8), :]
            compact = jnp.where(lane == i, pltpu.roll(x, i, 1) if i else x, compact)
    csend[...] = compact

    def fold(x):
        total = x[0:8]
        for v in range(1, nv):
            total = total + x[v * 8 : v * 8 + 8]
        return total

    vels = [jnp.where(live_f, vel_ref[c], 0.0) for c in range(3)]
    lines = [jnp.sum(fold(vels[a] * vels[b]), axis=0, keepdims=True) for a, b in PAIRS]
    lines.append(jnp.sum(fold(live_f.astype(jnp.float32)), axis=0, keepdims=True))
    lines.append(jnp.zeros((1, Z), jnp.float32))
    stat[pl.ds(8, 8), :] = jnp.concatenate(lines, axis=0)
    accA[...] = jnp.zeros(accA.shape, jnp.float32)
    vacc[...] = jnp.zeros(vacc.shape, jnp.float32)

    def pair_rows(j, h, theta_of, self_tile):
        base = pl.multiple_of(h * 16, 16)
        src = V if self_tile else oth
        other = [src[j, c, pl.ds(base, 16), :].reshape(2, 8, Z) for c in range(6)]
        B = [jnp.zeros((2, 8, Z), jnp.float32) for _ in range(3)]
        for s in range(slots):
            theta = theta_of(s, base).reshape(2, 8, Z)
            mine = [own[s, c] for c in range(6)]
            sep = [mine[c][None] - other[c] for c in range(3)]
            rel = [mine[3 + c][None] - other[3 + c] for c in range(3)]
            dist2 = sep[0] * sep[0] + sep[1] * sep[1] + sep[2] * sep[2]
            if self_tile:
                pos = lax.broadcasted_iota(jnp.int32, (2, 8, Z), 0) * 8
                pos = pos + lax.broadcasted_iota(jnp.int32, (2, 8, Z), 1) + h * 16
                dist2 = jnp.where(pos // Y == s, 4.0, dist2)
            inv = lax.rsqrt(dist2)
            w = jnp.maximum(1.0 - dist2 * inv, 0.0)
            closing = (sep[0] * rel[0] + sep[1] * rel[1] + sep[2] * rel[2]) * inv
            f = w * (REPULSION + NOISE_SCALE * theta - w * closing) * inv
            for c in range(3):
                F = f * sep[c]
                if not self_tile:
                    B[c] = B[c] + F
                accA[s, c] = accA[s, c] + (F[0] + F[1])
        if not self_tile:
            for c in range(3):
                Bs[j, c, pl.ds(base, 16), :] = B[c].reshape(16, Z)
            for q, (a, b) in enumerate(PAIRS):
                m = other[a] * B[b]
                vacc[q] = vacc[q] - (m[0] + m[1])

    loads[3].wait()
    for t in range(slots):
        x = nz[0, t].astype(jnp.float32)
        for s in range(slots):
            n0[s, pl.ds(t * Y, Y), :] = x[s * Y : s * Y + Y]

    def self_loop(h, carry):
        def theta_of(s, base):
            straight = nz[0, s, pl.ds(base, 16), :].astype(jnp.float32)
            return (straight + n0[s, pl.ds(base, 16), :]) * 0.7071067811865476

        pair_rows(0, h, theta_of, True)
        return carry

    lax.fori_loop(0, rows // 16, self_loop, 0)

    pl.semaphore_wait(barrier, len(partners))

    count = [0]

    def send(src, dst, e):
        i = count[0]
        count[0] += 1
        copy = pltpu.make_async_remote_copy(
            src_ref=src, dst_ref=dst, send_sem=ssem.at[i], recv_sem=rsem.at[i],
            device_id=dev(e), device_id_type=MESH,
        )
        copy.start()
        return copy

    halo = {g: [] for g in range(ng)}
    for g, (ex, _) in enumerate(groups):
        for e in (0, 1, -1):
            halo[g].append(send(csend, crecv.at[g, e + 1], (-ex, -e, -1)))
    for g, (ex, _) in enumerate(groups):
        if g:
            halo[g].append(send(V.at[0], V.at[g], (-ex, 0, 0)))
    for g, (ex, _) in enumerate(groups):
        halo[g].append(send(ysend.at[1], yrecv.at[g, 1], (-ex, -1, 0)))
        halo[g].append(send(ysend.at[0], yrecv.at[g, 0], (-ex, 1, 0)))
    every = [copy for g in range(ng) for copy in halo[g]]
    loads[4].wait()

    def send_sums():
        lines = []
        for q, (a, b) in enumerate(PAIRS):
            total = vacc[q]
            for s in range(slots):
                total = total + own[s, a] * accA[s, b]
            lines.append(jnp.sum(total, axis=0, keepdims=True))
        lines.append(jnp.zeros((2, Z), jnp.float32))
        stat[pl.ds(0, 8), :] = jnp.concatenate(lines, axis=0)
        column = jnp.sum(stat[...], axis=1, keepdims=True)
        r16 = lax.broadcasted_iota(jnp.int32, (16, Z), 0)
        l16 = lax.broadcasted_iota(jnp.int32, (16, Z), 1)
        line = jnp.sum(jnp.where(r16 == l16, jnp.broadcast_to(column, (16, Z)), 0.0), axis=0, keepdims=True)
        row_send[...] = jnp.broadcast_to(line, (8, Z))
        row_recv[here] = jnp.broadcast_to(line, (8, Z))
        return [
            send(row_send.at[pl.ds(0, 1)], row_recv.at[here, pl.ds(0, 1)], e) for e in phases[0] if e != (0, 0, 0)
        ]

    one_phase = len(phases) == 1
    here = me[0] * ny + me[1]
    if one_phase:
        here = here * nz_dev + me[2]
    returns = []
    for g, (ex, dxs) in enumerate(groups):
        for copy in halo[g]:
            copy.wait_recv()
        for first, dx in enumerate(dxs):
            tiles = tiles_of(dx)
            C = crecv[g, 1]
            CG = jnp.where(
                row_y == Y - 1, pltpu.roll(crecv[g, 2], Y - 1, 0), pltpu.roll(crecv[g, 0], 8 - (Y - 1), 0)
            )
            for c in range(6):
                Gy[c, pl.ds(Y - 1, slots, stride=Y), :] = yrecv[g, 1, c]
                Gy[c, pl.ds(0, slots, stride=Y), :] = yrecv[g, 0, c]

            def zshift(x, col, c):
                edge = jnp.concatenate(
                    [pltpu.roll(col, Z - 1 - (c * nv + v), 1) for v in range(nv)], axis=0
                )
                return jnp.where(lane_f == Z - 1, edge, pltpu.roll(x, Z - 1, 1))

            for c in range(6):
                x0, g0 = V[g, c], Gy[c]
                x1, g1 = zshift(x0, C, c), zshift(g0, CG, c)
                for j, (k, d) in enumerate(tiles):
                    x, gh = (x1, g1) if d[2] else (x0, g0)
                    if d[1] == 1:
                        x = jnp.where(rowy_f == Y - 1, gh, pltpu.roll(x, rows - 1, 0))
                    elif d[1] == -1:
                        x = jnp.where(rowy_f == 0, gh, pltpu.roll(x, 1, 0))
                    if c < 3 and d[c]:
                        x = x + float(d[c])
                    oth[j, c] = x

            k0, step = tiles[0][0], tiles[1][0] - tiles[0][0]

            def tile_loop(i, carry, k0=k0, step=step):
                j = i // (rows // 16)
                h = i - j * (rows // 16)
                k = k0 + step * j

                def theta_of(s, base):
                    return nz[k, s, pl.ds(base, 16), :].astype(jnp.float32)

                pair_rows(j, h, theta_of, False)
                return carry

            lax.fori_loop(0, len(tiles) * (rows // 16), tile_loop, 0)

            if g == ng - 1 and dx == dxs[-1]:
                sums = send_sums()

            RC = jnp.zeros((8, Z), jnp.float32)
            RCG = jnp.zeros((8, Z), jnp.float32)
            for b in range(3):
                loc, gho = [0.0, 0.0], [0.0, 0.0]
                for j, (k, d) in enumerate(tiles):
                    x = Bs[j, b]
                    z = d[2]
                    if d[1] == 0:
                        loc[z] = loc[z] + x
                    elif d[1] == 1:
                        loc[z] = loc[z] + jnp.where(rowy_f == 0, 0.0, pltpu.roll(x, 1, 0))
                        gho[z] = gho[z] + jnp.where(rowy_f == Y - 1, x, 0.0)
                    else:
                        loc[z] = loc[z] + jnp.where(rowy_f == Y - 1, 0.0, pltpu.roll(x, rows - 1, 0))
                        gho[z] = gho[z] + jnp.where(rowy_f == 0, x, 0.0)
                lz, gz = pltpu.roll(loc[1], 1, 1), pltpu.roll(gho[1], 1, 1)
                total = loc[0] + jnp.where(lane_f == 0, 0.0, lz)
                gtotal = gho[0] + jnp.where(lane_f == 0, 0.0, gz)
                if first:
                    total = total + R[g, b]
                    gtotal = gtotal + Gacc[b]
                R[g, b] = total
                Gacc[b] = gtotal
                for v in range(nv):
                    i = b * nv + v
                    xl, xg = lz[v * 8 : v * 8 + 8], gz[v * 8 : v * 8 + 8]
                    RC = jnp.where(lane == i, pltpu.roll(xl, i, 1) if i else xl, RC)
                    RCG = jnp.where(lane == i, pltpu.roll(xg, i, 1) if i else xg, RCG)
            if first:
                RC = RC + RCsend[g, 0]
                RCG = RCG + RCsend[g, 1]
            RCsend[g, 0] = RC
            RCsend[g, 1] = RCG
        for b in range(3):
            RGsend[g, 1, b] = Gacc[b, pl.ds(Y - 1, slots, stride=Y), :]
            RGsend[g, 0, b] = Gacc[b, pl.ds(0, slots, stride=Y), :]
        if g:
            returns.append(send(R.at[g], Rrecv.at[g], (ex, 0, 0)))
        returns.append(send(RGsend.at[g, 1], RGrecv.at[g, 1], (ex, 1, 0)))
        returns.append(send(RGsend.at[g, 0], RGrecv.at[g, 0], (ex, -1, 0)))
        for e in (-1, 0, 1):
            returns.append(send(RCsend.at[g, 0 if e == 0 else 1], RCrecv.at[g, e + 1], (ex, e, 1)))

    for b in range(3):
        packed = []
        for v in range(nv):
            out = None
            for u in range(G):
                x = accA[v * G + u, b]
                y = x
                for r in range(1, G):
                    y = y + pltpu.roll(x, r * Y, 0)
                out = y if out is None else jnp.where(row // Y == u, y, out)
            packed.append(out)
        R[0, b] = jnp.concatenate(packed, axis=0) - R[0, b]

    last = []
    if not one_phase:
        for copy in sums:
            copy.wait_recv()
        plane = row_recv[0]
        for i in range(1, nx * ny):
            plane = plane + row_recv[i]
        plane_send[...] = plane
        plane_recv[me[2]] = plane
        for e in phases[1]:
            if e != (0, 0, 0):
                last.append(send(plane_send, plane_recv.at[me[2]], e))

    for copy in returns:
        copy.wait_recv()
    corner = jnp.zeros((8, Z), jnp.float32)
    for g in range(ng):
        corner = corner + RCrecv[g, 1]
        corner = corner + jnp.where(row_y == 0, pltpu.roll(RCrecv[g, 0 + 2], 8 - (Y - 1), 0), 0.0)
        corner = corner + jnp.where(row_y == Y - 1, pltpu.roll(RCrecv[g, 0], Y - 1, 0), 0.0)
    for b in range(3):
        low = RGrecv[0, 1, b]
        high = RGrecv[0, 0, b]
        for g in range(1, ng):
            low = low + RGrecv[g, 1, b]
            high = high + RGrecv[g, 0, b]
        R[0, b, pl.ds(0, slots, stride=Y), :] = R[0, b, pl.ds(0, slots, stride=Y), :] - low
        R[0, b, pl.ds(Y - 1, slots, stride=Y), :] = R[0, b, pl.ds(Y - 1, slots, stride=Y), :] - high
        edge = jnp.concatenate(
            [pltpu.roll(corner, (Z - (b * nv + v)) % Z, 1) if b + v else corner for v in range(nv)], axis=0
        )
        total = R[0, b] - jnp.where(lane_f == 0, edge, 0.0)
        for g in range(1, ng):
            total = total - Rrecv[g, b]
        push_ref[b] = total

    for copy in sums if one_phase else last:
        copy.wait_recv()
    source, parts = (row_recv, nx * ny * nz_dev) if one_phase else (plane_recv, nz_dev)
    terms = [source[i, pl.ds(0, 1), :] for i in range(parts)]
    while len(terms) > 1:
        odd = terms[len(terms) // 2 * 2 :]
        terms = [terms[i] + terms[i + 1] for i in range(0, len(terms) - 1, 2)] + odd
    total = terms[0]
    total_ref[...] = jnp.broadcast_to(total, (8, Z))
    for copy in every + returns + sums + last:
        copy.wait_send()


def per_device(sizes, offset, velocity, occupancy, noise):
    slots, size_x, Y, Z = offset.shape[1:]
    assert size_x == 1 and slots == 8 and 8 % Y == 0 and Y > 1 and (slots * Y) % 16 == 0
    nx, ny, nzd = sizes
    rows = slots * Y
    ng = len(groups_of(nx))
    f32 = jnp.float32
    phases = phases_of(sizes)
    copies = (ng * 5 + ng - 1) * 2 + sum(len(phase) - 1 for phase in phases)
    vm = lambda *shape: pltpu.VMEM(shape, f32)
    spec = pl.BlockSpec(memory_space=pltpu.VMEM)
    outs = (
        jax.ShapeDtypeStruct((3, rows, Z), f32),
        jax.ShapeDtypeStruct((3, 3), f32),
        jax.ShapeDtypeStruct((1, 1), f32),
    )
    results = pl.pallas_call(
        functools.partial(kernel, sizes, slots, Y),
        out_shape=(vm(3, rows, Z), vm(8, Z)),
        in_specs=[pl.BlockSpec(memory_space=pl.ANY)] * 4,
        out_specs=(spec, spec),
        scratch_shapes=[
            vm(3, rows, Z),
            vm(3, rows, Z),
            pltpu.VMEM((Y, Z), jnp.int32),
            pltpu.VMEM((14, slots, rows, Z), jnp.bfloat16),
            vm(slots, rows, Z),
            vm(slots, 6, 8, Z),
            vm(ng, 6, rows, Z),
            vm(2, 6, slots, Z),
            vm(ng, 2, 6, slots, Z),
            vm(6, rows, Z),
            vm(8, Z),
            vm(ng, 3, 8, Z),
            vm(5, 6, rows, Z),
            vm(5, 3, rows, Z),
            vm(slots, 3, 8, Z),
            vm(6, 8, Z),
            vm(ng, 3, rows, Z),
            vm(ng, 3, rows, Z),
            vm(3, rows, Z),
            vm(ng, 2, 3, slots, Z),
            vm(ng, 2, 3, slots, Z),
            vm(ng, 2, 8, Z),
            vm(ng, 3, 8, Z),
            vm(16, Z),
            vm(8, Z),
            vm(len(phases[0]), 8, Z),
            vm(8, Z),
            vm(nzd, 8, Z),
            pltpu.SemaphoreType.DMA((5,)),
            pltpu.SemaphoreType.DMA((copies,)),
            pltpu.SemaphoreType.DMA((copies,)),
        ],
        compiler_params=pltpu.CompilerParams(collective_id=0, has_side_effects=True),
    )(
        offset.reshape(3, rows, Z),
        velocity.reshape(3, rows, Z),
        occupancy.reshape(Y, Z),
        noise.reshape(14, slots, rows, Z),
    )
    push, stress, thermal = pl.pallas_call(
        functools.partial(finish, Y * Z * nx * ny * nzd), out_shape=outs, in_specs=[spec] * 2, out_specs=(spec, spec, spec)
    )(*[pltpu.with_memory_space_constraint(r, pltpu.VMEM) for r in results])
    return push.reshape(offset.shape), stress, thermal.reshape(1)


def solution(mesh):
    placed = (
        P(None, None, "gx", "gy", "gz"),
        P(None, None, "gx", "gy", "gz"),
        P("gx", "gy", "gz"),
        P(None, None, None, "gx", "gy", "gz"),
    )
    sizes = tuple(mesh.shape[a] for a in ("gx", "gy", "gz"))
    return jax.shard_map(
        functools.partial(per_device, sizes),
        mesh=mesh,
        in_specs=placed,
        out_specs=(P(None, None, "gx", "gy", "gz"), P(), P()),
        check_vma=False,
    )
```

```python
import functools
import jax
import jax.numpy as jnp
from jax import lax
from jax.experimental import pallas as pl
from jax.experimental.pallas import tpu as pltpu
from jax.sharding import PartitionSpec as P

REPULSION = 25.0
FRICTION = 4.5
NOISE_SCALE = 15.0
FAR = 64.0
PAIRS = ((0, 0), (0, 1), (0, 2), (1, 1), (1, 2), (2, 2))
forward_shifts = [(1, 0, 0), (-1, 1, 0), (0, 1, 0), (1, 1, 0)] + [
    (dx, dy, 1) for dy in (-1, 0, 1) for dx in (-1, 0, 1)
]
MESH = pl.DeviceIdType.MESH


def tiles_of(dx):
    return [(k + 1, d) for k, d in enumerate(forward_shifts) if d[0] == dx]


def groups_of(nx):
    if nx == 2:
        return [(0, (0,)), (1, (1, -1))]
    return [(0, (0,)), (1, (1,)), (-1, (-1,))]


def phases_of(sizes):
    nx, ny, nz_dev = sizes
    plane = [(ex, ey, 0) for ex in range(nx) for ey in range(ny)]
    if nx * ny * nz_dev <= 64:
        return [[(ex, ey, ez) for ez in range(nz_dev) for ex, ey, _ in plane]]
    return [plane, [(0, 0, ez) for ez in range(nz_dev)]]


def finish(volume, push_in, total_in, push, stress, thermal):
    push[...] = push_in[...]
    total = total_in[0:1, :]
    item = lambda i: total[:, i : i + 1]
    r3 = lax.broadcasted_iota(jnp.int32, (3, 3), 0)
    c3 = lax.broadcasted_iota(jnp.int32, (3, 3), 1)
    matrix = jnp.zeros((3, 3), jnp.float32)
    for q, (a, b) in enumerate(PAIRS):
        hit = ((r3 == a) & (c3 == b)) | ((r3 == b) & (c3 == a))
        val = jnp.broadcast_to(item(8 + q) + item(q), (3, 3))
        matrix = jnp.where(hit, val, matrix)
    stress[...] = matrix / volume
    thermal[...] = (item(8) + item(11) + item(13)) / (3.0 * item(14) - 3.0)


def kernel(
    sizes, slots, Y,
    off_hbm, vel_hbm, occ_hbm, noise_ref,
    push_ref, total_ref,
    off_ref, vel_ref, occ_ref, nz, n0, own, V, ysend, yrecv, Gy, csend, crecv, oth, Bs, accA, vacc,
    R, Rrecv, Gacc, RGsend, RGrecv, RCsend, RCrecv, stat, row_send, row_recv, plane_send, plane_recv,
    nsem, ssem, rsem,
):
    nx, ny, nz_dev = sizes
    rows = slots * Y
    Z = off_ref.shape[2]
    G = 8 // Y
    nv = rows // 8
    groups = groups_of(nx)
    ng = len(groups)
    me = (lax.axis_index("gx"), lax.axis_index("gy"), lax.axis_index("gz"))

    def dev(e):
        return tuple(lax.rem(m + (o % n), n) for m, o, n in zip(me, e, sizes))

    partners = set()
    for ex, _ in groups:
        for ey in (-1, 0, 1):
            for ez in (-1, 0, 1):
                partners.add((ex % nx, ey % ny, ez % nz_dev))
                partners.add((-ex % nx, ey % ny, ez % nz_dev))
    phases = phases_of(sizes)
    for phase in phases:
        partners.update(phase)
    partners.discard((0, 0, 0))
    partners = sorted(partners)
    barrier = pltpu.get_barrier_semaphore()
    for e in partners:
        pl.semaphore_signal(barrier, inc=1, device_id=dev(e), device_id_type=MESH)

    loads = [
        pltpu.make_async_copy(off_hbm, off_ref, nsem.at[0]),
        pltpu.make_async_copy(vel_hbm, vel_ref, nsem.at[1]),
        pltpu.make_async_copy(occ_hbm, occ_ref, nsem.at[2]),
        pltpu.make_async_copy(noise_ref.at[0], nz.at[0], nsem.at[3]),
        pltpu.make_async_copy(noise_ref.at[pl.ds(1, 13)], nz.at[pl.ds(1, 13)], nsem.at[4]),
    ]
    for load in loads:
        load.start()

    lane = lax.broadcasted_iota(jnp.int32, (8, Z), 1)
    row = lax.broadcasted_iota(jnp.int32, (8, Z), 0)
    row_y = lax.rem(row, Y)
    lane_f = lax.broadcasted_iota(jnp.int32, (rows, Z), 1)
    row_f = lax.broadcasted_iota(jnp.int32, (rows, Z), 0)
    rowy_f = lax.rem(row_f, Y)
    slot_f = row_f // Y

    for load in loads[:3]:
        load.wait()
    occ = occ_ref[...]
    occ8 = jnp.concatenate([occ] * G, axis=0)
    occ_f = jnp.concatenate([occ8] * nv, axis=0)
    live_f = slot_f < occ_f
    for c in range(3):
        x = off_ref[c]
        if c == 0:
            V[0, 0] = jnp.where(live_f, x, FAR)
        else:
            V[0, c] = x
        V[0, 3 + c] = vel_ref[c] * FRICTION
    for s in range(slots):
        for c in range(3):
            x = off_ref[c, pl.ds(s * Y, Y), :]
            x = jnp.concatenate([x] * G, axis=0)
            if c == 0:
                x = jnp.where(occ8 > s, x, -FAR)
            own[s, c] = x
            v = vel_ref[c, pl.ds(s * Y, Y), :] * FRICTION
            own[s, 3 + c] = jnp.concatenate([v] * G, axis=0)
    compact = jnp.zeros((8, Z), jnp.float32)
    for c in range(6):
        ysend[0, c] = V[0, c, pl.ds(Y - 1, slots, stride=Y), :]
        ysend[1, c] = V[0, c, pl.ds(0, slots, stride=Y), :]
        for v in range(nv):
            i = c * nv + v
            x = V[0, c, pl.ds(v * 8, 8), :]
            compact = jnp.where(lane == i, pltpu.roll(x, i, 1) if i else x, compact)
    csend[...] = compact

    def fold(x):
        total = x[0:8]
        for v in range(1, nv):
            total = total + x[v * 8 : v * 8 + 8]
        return total

    vels = [jnp.where(live_f, vel_ref[c], 0.0) for c in range(3)]
    lines = [jnp.sum(fold(vels[a] * vels[b]), axis=0, keepdims=True) for a, b in PAIRS]
    lines.append(jnp.sum(fold(live_f.astype(jnp.float32)), axis=0, keepdims=True))
    lines.append(jnp.zeros((1, Z), jnp.float32))
    stat[pl.ds(8, 8), :] = jnp.concatenate(lines, axis=0)
    accA[...] = jnp.zeros(accA.shape, jnp.float32)
    vacc[...] = jnp.zeros(vacc.shape, jnp.float32)

    def pair_rows(j, h, theta_of, self_tile):
        base = pl.multiple_of(h * 16, 16)
        src = V if self_tile else oth
        other = [src[j, c, pl.ds(base, 16), :].reshape(2, 8, Z) for c in range(6)]
        B = [jnp.zeros((2, 8, Z), jnp.float32) for _ in range(3)]
        for s in range(slots):
            theta = theta_of(s, base).reshape(2, 8, Z)
            mine = [own[s, c] for c in range(6)]
            sep = [mine[c][None] - other[c] for c in range(3)]
            rel = [mine[3 + c][None] - other[3 + c] for c in range(3)]
            dist2 = sep[0] * sep[0] + sep[1] * sep[1] + sep[2] * sep[2]
            if self_tile:
                pos = lax.broadcasted_iota(jnp.int32, (2, 8, Z), 0) * 8
                pos = pos + lax.broadcasted_iota(jnp.int32, (2, 8, Z), 1) + h * 16
                dist2 = jnp.where(pos // Y == s, 4.0, dist2)
            inv = lax.rsqrt(dist2)
            w = jnp.maximum(1.0 - dist2 * inv, 0.0)
            closing = (sep[0] * rel[0] + sep[1] * rel[1] + sep[2] * rel[2]) * inv
            f = w * (REPULSION + NOISE_SCALE * theta - w * closing) * inv
            for c in range(3):
                F = f * sep[c]
                if not self_tile:
                    B[c] = B[c] + F
                accA[s, c] = accA[s, c] + (F[0] + F[1])
        if not self_tile:
            for c in range(3):
                Bs[j, c, pl.ds(base, 16), :] = B[c].reshape(16, Z)
            for q, (a, b) in enumerate(PAIRS):
                m = other[a] * B[b]
                vacc[q] = vacc[q] - (m[0] + m[1])

    loads[3].wait()
    for t in range(slots):
        x = nz[0, t].astype(jnp.float32)
        for s in range(slots):
            n0[s, pl.ds(t * Y, Y), :] = x[s * Y : s * Y + Y]

    def self_loop(h, carry):
        def theta_of(s, base):
            straight = nz[0, s, pl.ds(base, 16), :].astype(jnp.float32)
            return (straight + n0[s, pl.ds(base, 16), :]) * 0.7071067811865476

        pair_rows(0, h, theta_of, True)
        return carry

    lax.fori_loop(0, rows // 16, self_loop, 0)

    pl.semaphore_wait(barrier, len(partners))

    count = [0]

    def send(src, dst, e):
        i = count[0]
        count[0] += 1
        copy = pltpu.make_async_remote_copy(
            src_ref=src, dst_ref=dst, send_sem=ssem.at[i], recv_sem=rsem.at[i],
            device_id=dev(e), device_id_type=MESH,
        )
        copy.start()
        return copy

    halo = {g: [] for g in range(ng)}
    for g, (ex, _) in enumerate(groups):
        for e in (0, 1, -1):
            halo[g].append(send(csend, crecv.at[g, e + 1], (-ex, -e, -1)))
    for g, (ex, _) in reversed(list(enumerate(groups))):
        halo[g].append(send(ysend.at[1], yrecv.at[g, 1], (-ex, -1, 0)))
        halo[g].append(send(ysend.at[0], yrecv.at[g, 0], (-ex, 1, 0)))
    for g, (ex, _) in enumerate(groups):
        if g:
            halo[g].append(send(V.at[0], V.at[g], (-ex, 0, 0)))
    every = [copy for g in range(ng) for copy in halo[g]]
    loads[4].wait()

    def send_sums():
        lines = []
        for q, (a, b) in enumerate(PAIRS):
            total = vacc[q]
            for s in range(slots):
                total = total + own[s, a] * accA[s, b]
            lines.append(jnp.sum(total, axis=0, keepdims=True))
        lines.append(jnp.zeros((2, Z), jnp.float32))
        stat[pl.ds(0, 8), :] = jnp.concatenate(lines, axis=0)
        column = jnp.sum(stat[...], axis=1, keepdims=True)
        r16 = lax.broadcasted_iota(jnp.int32, (16, Z), 0)
        l16 = lax.broadcasted_iota(jnp.int32, (16, Z), 1)
        line = jnp.sum(jnp.where(r16 == l16, jnp.broadcast_to(column, (16, Z)), 0.0), axis=0, keepdims=True)
        row_send[...] = jnp.broadcast_to(line, (8, Z))
        row_recv[here] = jnp.broadcast_to(line, (8, Z))
        return [
            send(row_send.at[pl.ds(0, 1)], row_recv.at[here, pl.ds(0, 1)], e) for e in phases[0] if e != (0, 0, 0)
        ]

    one_phase = len(phases) == 1
    here = me[0] * ny + me[1]
    if one_phase:
        here = here * nz_dev + me[2]
    returns = []
    for g, (ex, dxs) in enumerate(groups):
        for copy in halo[g]:
            copy.wait_recv()
        for first, dx in enumerate(dxs):
            tiles = tiles_of(dx)
            C = crecv[g, 1]
            CG = jnp.where(
                row_y == Y - 1, pltpu.roll(crecv[g, 2], Y - 1, 0), pltpu.roll(crecv[g, 0], 8 - (Y - 1), 0)
            )
            for c in range(6):
                Gy[c, pl.ds(Y - 1, slots, stride=Y), :] = yrecv[g, 1, c]
                Gy[c, pl.ds(0, slots, stride=Y), :] = yrecv[g, 0, c]

            def zshift(x, col, c):
                edge = jnp.concatenate(
                    [pltpu.roll(col, Z - 1 - (c * nv + v), 1) for v in range(nv)], axis=0
                )
                return jnp.where(lane_f == Z - 1, edge, pltpu.roll(x, Z - 1, 1))

            for c in range(6):
                x0, g0 = V[g, c], Gy[c]
                x1, g1 = zshift(x0, C, c), zshift(g0, CG, c)
                for j, (k, d) in enumerate(tiles):
                    x, gh = (x1, g1) if d[2] else (x0, g0)
                    if d[1] == 1:
                        x = jnp.where(rowy_f == Y - 1, gh, pltpu.roll(x, rows - 1, 0))
                    elif d[1] == -1:
                        x = jnp.where(rowy_f == 0, gh, pltpu.roll(x, 1, 0))
                    if c < 3 and d[c]:
                        x = x + float(d[c])
                    oth[j, c] = x

            k0, step = tiles[0][0], tiles[1][0] - tiles[0][0]

            def tile_loop(i, carry, k0=k0, step=step):
                j = i // (rows // 16)
                h = i - j * (rows // 16)
                k = k0 + step * j

                def theta_of(s, base):
                    return nz[k, s, pl.ds(base, 16), :].astype(jnp.float32)

                pair_rows(j, h, theta_of, False)
                return carry

            lax.fori_loop(0, len(tiles) * (rows // 16), tile_loop, 0)

            if g == ng - 1 and dx == dxs[-1]:
                sums = send_sums()

            RC = jnp.zeros((8, Z), jnp.float32)
            RCG = jnp.zeros((8, Z), jnp.float32)
            for b in range(3):
                loc, gho = [0.0, 0.0], [0.0, 0.0]
                for j, (k, d) in enumerate(tiles):
                    x = Bs[j, b]
                    z = d[2]
                    if d[1] == 0:
                        loc[z] = loc[z] + x
                    elif d[1] == 1:
                        loc[z] = loc[z] + jnp.where(rowy_f == 0, 0.0, pltpu.roll(x, 1, 0))
                        gho[z] = gho[z] + jnp.where(rowy_f == Y - 1, x, 0.0)
                    else:
                        loc[z] = loc[z] + jnp.where(rowy_f == Y - 1, 0.0, pltpu.roll(x, rows - 1, 0))
                        gho[z] = gho[z] + jnp.where(rowy_f == 0, x, 0.0)
                lz, gz = pltpu.roll(loc[1], 1, 1), pltpu.roll(gho[1], 1, 1)
                total = loc[0] + jnp.where(lane_f == 0, 0.0, lz)
                gtotal = gho[0] + jnp.where(lane_f == 0, 0.0, gz)
                if first:
                    total = total + R[g, b]
                    gtotal = gtotal + Gacc[b]
                R[g, b] = total
                Gacc[b] = gtotal
                for v in range(nv):
                    i = b * nv + v
                    xl, xg = lz[v * 8 : v * 8 + 8], gz[v * 8 : v * 8 + 8]
                    RC = jnp.where(lane == i, pltpu.roll(xl, i, 1) if i else xl, RC)
                    RCG = jnp.where(lane == i, pltpu.roll(xg, i, 1) if i else xg, RCG)
            if first:
                RC = RC + RCsend[g, 0]
                RCG = RCG + RCsend[g, 1]
            RCsend[g, 0] = RC
            RCsend[g, 1] = RCG
        for b in range(3):
            RGsend[g, 1, b] = Gacc[b, pl.ds(Y - 1, slots, stride=Y), :]
            RGsend[g, 0, b] = Gacc[b, pl.ds(0, slots, stride=Y), :]
        if g:
            returns.append(send(R.at[g], Rrecv.at[g], (ex, 0, 0)))
        returns.append(send(RGsend.at[g, 1], RGrecv.at[g, 1], (ex, 1, 0)))
        returns.append(send(RGsend.at[g, 0], RGrecv.at[g, 0], (ex, -1, 0)))
        for e in (-1, 0, 1):
            returns.append(send(RCsend.at[g, 0 if e == 0 else 1], RCrecv.at[g, e + 1], (ex, e, 1)))

    for b in range(3):
        packed = []
        for v in range(nv):
            out = None
            for u in range(G):
                x = accA[v * G + u, b]
                y = x
                for r in range(1, G):
                    y = y + pltpu.roll(x, r * Y, 0)
                out = y if out is None else jnp.where(row // Y == u, y, out)
            packed.append(out)
        R[0, b] = jnp.concatenate(packed, axis=0) - R[0, b]

    last = []
    if not one_phase:
        for copy in sums:
            copy.wait_recv()
        plane = row_recv[0]
        for i in range(1, nx * ny):
            plane = plane + row_recv[i]
        plane_send[...] = plane
        plane_recv[me[2]] = plane
        for e in phases[1]:
            if e != (0, 0, 0):
                last.append(send(plane_send, plane_recv.at[me[2]], e))

    for copy in returns:
        copy.wait_recv()
    corner = jnp.zeros((8, Z), jnp.float32)
    for g in range(ng):
        corner = corner + RCrecv[g, 1]
        corner = corner + jnp.where(row_y == 0, pltpu.roll(RCrecv[g, 0 + 2], 8 - (Y - 1), 0), 0.0)
        corner = corner + jnp.where(row_y == Y - 1, pltpu.roll(RCrecv[g, 0], Y - 1, 0), 0.0)
    for b in range(3):
        low = RGrecv[0, 1, b]
        high = RGrecv[0, 0, b]
        for g in range(1, ng):
            low = low + RGrecv[g, 1, b]
            high = high + RGrecv[g, 0, b]
        R[0, b, pl.ds(0, slots, stride=Y), :] = R[0, b, pl.ds(0, slots, stride=Y), :] - low
        R[0, b, pl.ds(Y - 1, slots, stride=Y), :] = R[0, b, pl.ds(Y - 1, slots, stride=Y), :] - high
        edge = jnp.concatenate(
            [pltpu.roll(corner, (Z - (b * nv + v)) % Z, 1) if b + v else corner for v in range(nv)], axis=0
        )
        total = R[0, b] - jnp.where(lane_f == 0, edge, 0.0)
        for g in range(1, ng):
            total = total - Rrecv[g, b]
        push_ref[b] = total

    for copy in sums if one_phase else last:
        copy.wait_recv()
    source, parts = (row_recv, nx * ny * nz_dev) if one_phase else (plane_recv, nz_dev)
    terms = [source[i, pl.ds(0, 1), :] for i in range(parts)]
    while len(terms) > 1:
        odd = terms[len(terms) // 2 * 2 :]
        terms = [terms[i] + terms[i + 1] for i in range(0, len(terms) - 1, 2)] + odd
    total = terms[0]
    total_ref[...] = jnp.broadcast_to(total, (8, Z))
    for copy in every + returns + sums + last:
        copy.wait_send()


def per_device(sizes, offset, velocity, occupancy, noise):
    slots, size_x, Y, Z = offset.shape[1:]
    assert size_x == 1 and slots == 8 and 8 % Y == 0 and Y > 1 and (slots * Y) % 16 == 0
    nx, ny, nzd = sizes
    rows = slots * Y
    ng = len(groups_of(nx))
    f32 = jnp.float32
    phases = phases_of(sizes)
    copies = (ng * 5 + ng - 1) * 2 + sum(len(phase) - 1 for phase in phases)
    vm = lambda *shape: pltpu.VMEM(shape, f32)
    spec = pl.BlockSpec(memory_space=pltpu.VMEM)
    outs = (
        jax.ShapeDtypeStruct((3, rows, Z), f32),
        jax.ShapeDtypeStruct((3, 3), f32),
        jax.ShapeDtypeStruct((1, 1), f32),
    )
    results = pl.pallas_call(
        functools.partial(kernel, sizes, slots, Y),
        out_shape=(vm(3, rows, Z), vm(8, Z)),
        in_specs=[pl.BlockSpec(memory_space=pl.ANY)] * 4,
        out_specs=(spec, spec),
        scratch_shapes=[
            vm(3, rows, Z),
            vm(3, rows, Z),
            pltpu.VMEM((Y, Z), jnp.int32),
            pltpu.VMEM((14, slots, rows, Z), jnp.bfloat16),
            vm(slots, rows, Z),
            vm(slots, 6, 8, Z),
            vm(ng, 6, rows, Z),
            vm(2, 6, slots, Z),
            vm(ng, 2, 6, slots, Z),
            vm(6, rows, Z),
            vm(8, Z),
            vm(ng, 3, 8, Z),
            vm(5, 6, rows, Z),
            vm(5, 3, rows, Z),
            vm(slots, 3, 8, Z),
            vm(6, 8, Z),
            vm(ng, 3, rows, Z),
            vm(ng, 3, rows, Z),
            vm(3, rows, Z),
            vm(ng, 2, 3, slots, Z),
            vm(ng, 2, 3, slots, Z),
            vm(ng, 2, 8, Z),
            vm(ng, 3, 8, Z),
            vm(16, Z),
            vm(8, Z),
            vm(len(phases[0]), 8, Z),
            vm(8, Z),
            vm(nzd, 8, Z),
            pltpu.SemaphoreType.DMA((5,)),
            pltpu.SemaphoreType.DMA((copies,)),
            pltpu.SemaphoreType.DMA((copies,)),
        ],
        compiler_params=pltpu.CompilerParams(collective_id=0, has_side_effects=True),
    )(
        offset.reshape(3, rows, Z),
        velocity.reshape(3, rows, Z),
        occupancy.reshape(Y, Z),
        noise.reshape(14, slots, rows, Z),
    )
    push, stress, thermal = pl.pallas_call(
        functools.partial(finish, Y * Z * nx * ny * nzd), out_shape=outs, in_specs=[spec] * 2, out_specs=(spec, spec, spec)
    )(*[pltpu.with_memory_space_constraint(r, pltpu.VMEM) for r in results])
    return push.reshape(offset.shape), stress, thermal.reshape(1)


def solution(mesh):
    placed = (
        P(None, None, "gx", "gy", "gz"),
        P(None, None, "gx", "gy", "gz"),
        P("gx", "gy", "gz"),
        P(None, None, None, "gx", "gy", "gz"),
    )
    sizes = tuple(mesh.shape[a] for a in ("gx", "gy", "gz"))
    return jax.shard_map(
        functools.partial(per_device, sizes),
        mesh=mesh,
        in_specs=placed,
        out_specs=(P(None, None, "gx", "gy", "gz"), P(), P()),
        check_vma=False,
    )
```

```python
import functools
import jax
import jax.numpy as jnp
from jax import lax
from jax.experimental import pallas as pl
from jax.experimental.pallas import tpu as pltpu
from jax.sharding import PartitionSpec as P

REPULSION = 25.0
FRICTION = 4.5
NOISE_SCALE = 15.0
FAR = 64.0
TOP = 32767.0
PAIRS = ((0, 0), (0, 1), (0, 2), (1, 1), (1, 2), (2, 2))
forward_shifts = [(1, 0, 0), (-1, 1, 0), (0, 1, 0), (1, 1, 0)] + [
    (dx, dy, 1) for dy in (-1, 0, 1) for dx in (-1, 0, 1)
]
MESH = pl.DeviceIdType.MESH


def tiles_of(dx):
    return [(k + 1, d) for k, d in enumerate(forward_shifts) if d[0] == dx]


def groups_of(nx):
    if nx == 2:
        return [(0, (0,)), (1, (1, -1))]
    return [(0, (0,)), (1, (1,)), (-1, (-1,))]


def phases_of(sizes):
    nx, ny, nz_dev = sizes
    plane = [(ex, ey, 0) for ex in range(nx) for ey in range(ny)]
    if nx * ny * nz_dev <= 64:
        return [[(ex, ey, ez) for ez in range(nz_dev) for ex, ey, _ in plane]]
    return [plane, [(0, 0, ez) for ez in range(nz_dev)]]


def finish(volume, push_in, total_in, push, stress, thermal):
    push[...] = push_in[...]
    total = total_in[0:1, :]
    item = lambda i: total[:, i : i + 1]
    r3 = lax.broadcasted_iota(jnp.int32, (3, 3), 0)
    c3 = lax.broadcasted_iota(jnp.int32, (3, 3), 1)
    matrix = jnp.zeros((3, 3), jnp.float32)
    for q, (a, b) in enumerate(PAIRS):
        hit = ((r3 == a) & (c3 == b)) | ((r3 == b) & (c3 == a))
        val = jnp.broadcast_to(item(8 + q) + item(q), (3, 3))
        matrix = jnp.where(hit, val, matrix)
    stress[...] = matrix / volume
    thermal[...] = (item(8) + item(11) + item(13)) / (3.0 * item(14) - 3.0)


def kernel(
    sizes, slots, Y,
    off_hbm, vel_hbm, occ_hbm, noise_ref,
    push_ref, total_ref,
    off_ref, vel_ref, occ_ref, nz, n0, own, V, hsend, hrecv, ysend, yrecv, Gy, csend, crecv, oth, Bs, accA, vacc,
    R, Rrecv, Gacc, RGsend, RGrecv, RCsend, RCrecv, stat, row_send, row_recv, plane_send, plane_recv,
    nsem, ssem, rsem,
):
    nx, ny, nz_dev = sizes
    rows = slots * Y
    Z = off_ref.shape[2]
    G = 8 // Y
    nv = rows // 8
    groups = groups_of(nx)
    ng = len(groups)
    me = (lax.axis_index("gx"), lax.axis_index("gy"), lax.axis_index("gz"))

    def dev(e):
        return tuple(lax.rem(m + (o % n), n) for m, o, n in zip(me, e, sizes))

    partners = set()
    for ex, _ in groups:
        for ey in (-1, 0, 1):
            for ez in (-1, 0, 1):
                partners.add((ex % nx, ey % ny, ez % nz_dev))
                partners.add((-ex % nx, ey % ny, ez % nz_dev))
    phases = phases_of(sizes)
    for phase in phases:
        partners.update(phase)
    partners.discard((0, 0, 0))
    partners = sorted(partners)
    barrier = pltpu.get_barrier_semaphore()
    for e in partners:
        pl.semaphore_signal(barrier, inc=1, device_id=dev(e), device_id_type=MESH)

    loads = [
        pltpu.make_async_copy(off_hbm, off_ref, nsem.at[0]),
        pltpu.make_async_copy(vel_hbm, vel_ref, nsem.at[1]),
        pltpu.make_async_copy(occ_hbm, occ_ref, nsem.at[2]),
        pltpu.make_async_copy(noise_ref.at[0], nz.at[0], nsem.at[3]),
        pltpu.make_async_copy(noise_ref.at[pl.ds(1, 13)], nz.at[pl.ds(1, 13)], nsem.at[4]),
    ]
    for load in loads:
        load.start()

    lane = lax.broadcasted_iota(jnp.int32, (8, Z), 1)
    row = lax.broadcasted_iota(jnp.int32, (8, Z), 0)
    row_y = lax.rem(row, Y)
    lane_f = lax.broadcasted_iota(jnp.int32, (rows, Z), 1)
    row_f = lax.broadcasted_iota(jnp.int32, (rows, Z), 0)
    rowy_f = lax.rem(row_f, Y)
    slot_f = row_f // Y

    for load in loads[:3]:
        load.wait()
    occ = occ_ref[...]
    occ8 = jnp.concatenate([occ] * G, axis=0)
    occ_f = jnp.concatenate([occ8] * nv, axis=0)
    live_f = slot_f < occ_f
    for c in range(3):
        x = off_ref[c]
        if c == 0:
            V[0, 0] = jnp.where(live_f, x, FAR)
        else:
            V[0, c] = x
        V[0, 3 + c] = vel_ref[c] * FRICTION
        code = jnp.floor((x - 0.5) * (TOP / 0.45) + 0.5)
        code = jnp.clip(code, -TOP, TOP).astype(jnp.int32)
        if c == 0:
            code = jnp.where(live_f, code, -32768)
        hsend[c] = code.astype(jnp.int16)
        code = jnp.floor(vel_ref[c] * (TOP / 11.0) + 0.5)
        hsend[3 + c] = jnp.clip(code, -TOP, TOP).astype(jnp.int32).astype(jnp.int16)
    for s in range(slots):
        for c in range(3):
            x = off_ref[c, pl.ds(s * Y, Y), :]
            x = jnp.concatenate([x] * G, axis=0)
            if c == 0:
                x = jnp.where(occ8 > s, x, -FAR)
            own[s, c] = x
            v = vel_ref[c, pl.ds(s * Y, Y), :] * FRICTION
            own[s, 3 + c] = jnp.concatenate([v] * G, axis=0)
    compact = jnp.zeros((8, Z), jnp.float32)
    for c in range(6):
        ysend[0, c] = V[0, c, pl.ds(Y - 1, slots, stride=Y), :]
        ysend[1, c] = V[0, c, pl.ds(0, slots, stride=Y), :]
        for v in range(nv):
            i = c * nv + v
            x = V[0, c, pl.ds(v * 8, 8), :]
            compact = jnp.where(lane == i, pltpu.roll(x, i, 1) if i else x, compact)
    csend[...] = compact

    def fold(x):
        total = x[0:8]
        for v in range(1, nv):
            total = total + x[v * 8 : v * 8 + 8]
        return total

    vels = [jnp.where(live_f, vel_ref[c], 0.0) for c in range(3)]
    lines = [jnp.sum(fold(vels[a] * vels[b]), axis=0, keepdims=True) for a, b in PAIRS]
    lines.append(jnp.sum(fold(live_f.astype(jnp.float32)), axis=0, keepdims=True))
    lines.append(jnp.zeros((1, Z), jnp.float32))
    stat[pl.ds(8, 8), :] = jnp.concatenate(lines, axis=0)
    accA[...] = jnp.zeros(accA.shape, jnp.float32)
    vacc[...] = jnp.zeros(vacc.shape, jnp.float32)

    def pair_rows(j, h, theta_of, self_tile):
        base = pl.multiple_of(h * 16, 16)
        src = V if self_tile else oth
        other = [src[j, c, pl.ds(base, 16), :].reshape(2, 8, Z) for c in range(6)]
        B = [jnp.zeros((2, 8, Z), jnp.float32) for _ in range(3)]
        for s in range(slots):
            theta = theta_of(s, base).reshape(2, 8, Z)
            mine = [own[s, c] for c in range(6)]
            sep = [mine[c][None] - other[c] for c in range(3)]
            rel = [mine[3 + c][None] - other[3 + c] for c in range(3)]
            dist2 = sep[0] * sep[0] + sep[1] * sep[1] + sep[2] * sep[2]
            if self_tile:
                pos = lax.broadcasted_iota(jnp.int32, (2, 8, Z), 0) * 8
                pos = pos + lax.broadcasted_iota(jnp.int32, (2, 8, Z), 1) + h * 16
                dist2 = jnp.where(pos // Y == s, 4.0, dist2)
            inv = lax.rsqrt(dist2)
            w = jnp.maximum(1.0 - dist2 * inv, 0.0)
            closing = (sep[0] * rel[0] + sep[1] * rel[1] + sep[2] * rel[2]) * inv
            f = w * (REPULSION + NOISE_SCALE * theta - w * closing) * inv
            for c in range(3):
                F = f * sep[c]
                if not self_tile:
                    B[c] = B[c] + F
                accA[s, c] = accA[s, c] + (F[0] + F[1])
        if not self_tile:
            for c in range(3):
                Bs[j, c, pl.ds(base, 16), :] = B[c].reshape(16, Z)
            for q, (a, b) in enumerate(PAIRS):
                m = other[a] * B[b]
                vacc[q] = vacc[q] - (m[0] + m[1])

    loads[3].wait()
    for t in range(slots):
        x = nz[0, t].astype(jnp.float32)
        for s in range(slots):
            n0[s, pl.ds(t * Y, Y), :] = x[s * Y : s * Y + Y]

    def self_loop(h, carry):
        def theta_of(s, base):
            straight = nz[0, s, pl.ds(base, 16), :].astype(jnp.float32)
            return (straight + n0[s, pl.ds(base, 16), :]) * 0.7071067811865476

        pair_rows(0, h, theta_of, True)
        return carry

    lax.fori_loop(0, rows // 16, self_loop, 0)

    pl.semaphore_wait(barrier, len(partners))

    count = [0]

    def send(src, dst, e):
        i = count[0]
        count[0] += 1
        copy = pltpu.make_async_remote_copy(
            src_ref=src, dst_ref=dst, send_sem=ssem.at[i], recv_sem=rsem.at[i],
            device_id=dev(e), device_id_type=MESH,
        )
        copy.start()
        return copy

    halo = {g: [] for g in range(ng)}
    for g, (ex, _) in enumerate(groups):
        for e in (0, 1, -1):
            halo[g].append(send(csend, crecv.at[g, e + 1], (-ex, -e, -1)))
    for g, (ex, _) in reversed(list(enumerate(groups))):
        halo[g].append(send(ysend.at[1], yrecv.at[g, 1], (-ex, -1, 0)))
        halo[g].append(send(ysend.at[0], yrecv.at[g, 0], (-ex, 1, 0)))
    for g, (ex, _) in enumerate(groups):
        if g:
            halo[g].append(send(hsend, hrecv.at[g], (-ex, 0, 0)))
    every = [copy for g in range(ng) for copy in halo[g]]
    loads[4].wait()

    def send_sums():
        lines = []
        for q, (a, b) in enumerate(PAIRS):
            total = vacc[q]
            for s in range(slots):
                total = total + own[s, a] * accA[s, b]
            lines.append(jnp.sum(total, axis=0, keepdims=True))
        lines.append(jnp.zeros((2, Z), jnp.float32))
        stat[pl.ds(0, 8), :] = jnp.concatenate(lines, axis=0)
        column = jnp.sum(stat[...], axis=1, keepdims=True)
        r16 = lax.broadcasted_iota(jnp.int32, (16, Z), 0)
        l16 = lax.broadcasted_iota(jnp.int32, (16, Z), 1)
        line = jnp.sum(jnp.where(r16 == l16, jnp.broadcast_to(column, (16, Z)), 0.0), axis=0, keepdims=True)
        row_send[...] = jnp.broadcast_to(line, (8, Z))
        row_recv[here] = jnp.broadcast_to(line, (8, Z))
        return [
            send(row_send.at[pl.ds(0, 1)], row_recv.at[here, pl.ds(0, 1)], e) for e in phases[0] if e != (0, 0, 0)
        ]

    one_phase = len(phases) == 1
    here = me[0] * ny + me[1]
    if one_phase:
        here = here * nz_dev + me[2]
    returns = []
    for g, (ex, dxs) in enumerate(groups):
        for copy in halo[g]:
            copy.wait_recv()
        if g:
            for c in range(3):
                code = hrecv[g, c].astype(jnp.int32)
                x = code.astype(jnp.float32) * (0.45 / TOP) + 0.5
                V[g, c] = jnp.where(code == -32768, FAR, x) if c == 0 else x
                code = hrecv[g, 3 + c].astype(jnp.int32)
                V[g, 3 + c] = code.astype(jnp.float32) * (11.0 * FRICTION / TOP)
        for first, dx in enumerate(dxs):
            tiles = tiles_of(dx)
            C = crecv[g, 1]
            CG = jnp.where(
                row_y == Y - 1, pltpu.roll(crecv[g, 2], Y - 1, 0), pltpu.roll(crecv[g, 0], 8 - (Y - 1), 0)
            )
            for c in range(6):
                Gy[c, pl.ds(Y - 1, slots, stride=Y), :] = yrecv[g, 1, c]
                Gy[c, pl.ds(0, slots, stride=Y), :] = yrecv[g, 0, c]

            def zshift(x, col, c):
                edge = jnp.concatenate(
                    [pltpu.roll(col, Z - 1 - (c * nv + v), 1) for v in range(nv)], axis=0
                )
                return jnp.where(lane_f == Z - 1, edge, pltpu.roll(x, Z - 1, 1))

            for c in range(6):
                x0, g0 = V[g, c], Gy[c]
                x1, g1 = zshift(x0, C, c), zshift(g0, CG, c)
                for j, (k, d) in enumerate(tiles):
                    x, gh = (x1, g1) if d[2] else (x0, g0)
                    if d[1] == 1:
                        x = jnp.where(rowy_f == Y - 1, gh, pltpu.roll(x, rows - 1, 0))
                    elif d[1] == -1:
                        x = jnp.where(rowy_f == 0, gh, pltpu.roll(x, 1, 0))
                    if c < 3 and d[c]:
                        x = x + float(d[c])
                    oth[j, c] = x

            k0, step = tiles[0][0], tiles[1][0] - tiles[0][0]

            def tile_loop(i, carry, k0=k0, step=step):
                j = i // (rows // 16)
                h = i - j * (rows // 16)
                k = k0 + step * j

                def theta_of(s, base):
                    return nz[k, s, pl.ds(base, 16), :].astype(jnp.float32)

                pair_rows(j, h, theta_of, False)
                return carry

            lax.fori_loop(0, len(tiles) * (rows // 16), tile_loop, 0)

            if g == ng - 1 and dx == dxs[-1]:
                sums = send_sums()

            RC = jnp.zeros((8, Z), jnp.float32)
            RCG = jnp.zeros((8, Z), jnp.float32)
            for b in range(3):
                loc, gho = [0.0, 0.0], [0.0, 0.0]
                for j, (k, d) in enumerate(tiles):
                    x = Bs[j, b]
                    z = d[2]
                    if d[1] == 0:
                        loc[z] = loc[z] + x
                    elif d[1] == 1:
                        loc[z] = loc[z] + jnp.where(rowy_f == 0, 0.0, pltpu.roll(x, 1, 0))
                        gho[z] = gho[z] + jnp.where(rowy_f == Y - 1, x, 0.0)
                    else:
                        loc[z] = loc[z] + jnp.where(rowy_f == Y - 1, 0.0, pltpu.roll(x, rows - 1, 0))
                        gho[z] = gho[z] + jnp.where(rowy_f == 0, x, 0.0)
                lz, gz = pltpu.roll(loc[1], 1, 1), pltpu.roll(gho[1], 1, 1)
                total = loc[0] + jnp.where(lane_f == 0, 0.0, lz)
                gtotal = gho[0] + jnp.where(lane_f == 0, 0.0, gz)
                if first:
                    total = total + R[g, b]
                    gtotal = gtotal + Gacc[b]
                R[g, b] = total
                Gacc[b] = gtotal
                for v in range(nv):
                    i = b * nv + v
                    xl, xg = lz[v * 8 : v * 8 + 8], gz[v * 8 : v * 8 + 8]
                    RC = jnp.where(lane == i, pltpu.roll(xl, i, 1) if i else xl, RC)
                    RCG = jnp.where(lane == i, pltpu.roll(xg, i, 1) if i else xg, RCG)
            if first:
                RC = RC + RCsend[g, 0]
                RCG = RCG + RCsend[g, 1]
            RCsend[g, 0] = RC
            RCsend[g, 1] = RCG
        for b in range(3):
            RGsend[g, 1, b] = Gacc[b, pl.ds(Y - 1, slots, stride=Y), :]
            RGsend[g, 0, b] = Gacc[b, pl.ds(0, slots, stride=Y), :]
        if g:
            returns.append(send(R.at[g], Rrecv.at[g], (ex, 0, 0)))
        returns.append(send(RGsend.at[g, 1], RGrecv.at[g, 1], (ex, 1, 0)))
        returns.append(send(RGsend.at[g, 0], RGrecv.at[g, 0], (ex, -1, 0)))
        for e in (-1, 0, 1):
            returns.append(send(RCsend.at[g, 0 if e == 0 else 1], RCrecv.at[g, e + 1], (ex, e, 1)))

    for b in range(3):
        packed = []
        for v in range(nv):
            out = None
            for u in range(G):
                x = accA[v * G + u, b]
                y = x
                for r in range(1, G):
                    y = y + pltpu.roll(x, r * Y, 0)
                out = y if out is None else jnp.where(row // Y == u, y, out)
            packed.append(out)
        R[0, b] = jnp.concatenate(packed, axis=0) - R[0, b]

    last = []
    if not one_phase:
        for copy in sums:
            copy.wait_recv()
        plane = row_recv[0]
        for i in range(1, nx * ny):
            plane = plane + row_recv[i]
        plane_send[...] = plane
        plane_recv[me[2]] = plane
        for e in phases[1]:
            if e != (0, 0, 0):
                last.append(send(plane_send, plane_recv.at[me[2]], e))

    for copy in returns:
        copy.wait_recv()
    corner = jnp.zeros((8, Z), jnp.float32)
    for g in range(ng):
        corner = corner + RCrecv[g, 1]
        corner = corner + jnp.where(row_y == 0, pltpu.roll(RCrecv[g, 0 + 2], 8 - (Y - 1), 0), 0.0)
        corner = corner + jnp.where(row_y == Y - 1, pltpu.roll(RCrecv[g, 0], Y - 1, 0), 0.0)
    for b in range(3):
        low = RGrecv[0, 1, b]
        high = RGrecv[0, 0, b]
        for g in range(1, ng):
            low = low + RGrecv[g, 1, b]
            high = high + RGrecv[g, 0, b]
        R[0, b, pl.ds(0, slots, stride=Y), :] = R[0, b, pl.ds(0, slots, stride=Y), :] - low
        R[0, b, pl.ds(Y - 1, slots, stride=Y), :] = R[0, b, pl.ds(Y - 1, slots, stride=Y), :] - high
        edge = jnp.concatenate(
            [pltpu.roll(corner, (Z - (b * nv + v)) % Z, 1) if b + v else corner for v in range(nv)], axis=0
        )
        total = R[0, b] - jnp.where(lane_f == 0, edge, 0.0)
        for g in range(1, ng):
            total = total - Rrecv[g, b]
        push_ref[b] = total

    for copy in sums if one_phase else last:
        copy.wait_recv()
    source, parts = (row_recv, nx * ny * nz_dev) if one_phase else (plane_recv, nz_dev)
    terms = [source[i, pl.ds(0, 1), :] for i in range(parts)]
    while len(terms) > 1:
        odd = terms[len(terms) // 2 * 2 :]
        terms = [terms[i] + terms[i + 1] for i in range(0, len(terms) - 1, 2)] + odd
    total = terms[0]
    total_ref[...] = jnp.broadcast_to(total, (8, Z))
    for copy in every + returns + sums + last:
        copy.wait_send()


def per_device(sizes, offset, velocity, occupancy, noise):
    slots, size_x, Y, Z = offset.shape[1:]
    assert size_x == 1 and slots == 8 and 8 % Y == 0 and Y > 1 and (slots * Y) % 16 == 0
    nx, ny, nzd = sizes
    rows = slots * Y
    ng = len(groups_of(nx))
    f32 = jnp.float32
    phases = phases_of(sizes)
    copies = (ng * 5 + ng - 1) * 2 + sum(len(phase) - 1 for phase in phases)
    vm = lambda *shape: pltpu.VMEM(shape, f32)
    spec = pl.BlockSpec(memory_space=pltpu.VMEM)
    outs = (
        jax.ShapeDtypeStruct((3, rows, Z), f32),
        jax.ShapeDtypeStruct((3, 3), f32),
        jax.ShapeDtypeStruct((1, 1), f32),
    )
    results = pl.pallas_call(
        functools.partial(kernel, sizes, slots, Y),
        out_shape=(vm(3, rows, Z), vm(8, Z)),
        in_specs=[pl.BlockSpec(memory_space=pl.ANY)] * 4,
        out_specs=(spec, spec),
        scratch_shapes=[
            vm(3, rows, Z),
            vm(3, rows, Z),
            pltpu.VMEM((Y, Z), jnp.int32),
            pltpu.VMEM((14, slots, rows, Z), jnp.bfloat16),
            vm(slots, rows, Z),
            vm(slots, 6, 8, Z),
            vm(ng, 6, rows, Z),
            pltpu.VMEM((6, rows, Z), jnp.int16),
            pltpu.VMEM((ng, 6, rows, Z), jnp.int16),
            vm(2, 6, slots, Z),
            vm(ng, 2, 6, slots, Z),
            vm(6, rows, Z),
            vm(8, Z),
            vm(ng, 3, 8, Z),
            vm(5, 6, rows, Z),
            vm(5, 3, rows, Z),
            vm(slots, 3, 8, Z),
            vm(6, 8, Z),
            vm(ng, 3, rows, Z),
            vm(ng, 3, rows, Z),
            vm(3, rows, Z),
            vm(ng, 2, 3, slots, Z),
            vm(ng, 2, 3, slots, Z),
            vm(ng, 2, 8, Z),
            vm(ng, 3, 8, Z),
            vm(16, Z),
            vm(8, Z),
            vm(len(phases[0]), 8, Z),
            vm(8, Z),
            vm(nzd, 8, Z),
            pltpu.SemaphoreType.DMA((5,)),
            pltpu.SemaphoreType.DMA((copies,)),
            pltpu.SemaphoreType.DMA((copies,)),
        ],
        compiler_params=pltpu.CompilerParams(collective_id=0, has_side_effects=True),
    )(
        offset.reshape(3, rows, Z),
        velocity.reshape(3, rows, Z),
        occupancy.reshape(Y, Z),
        noise.reshape(14, slots, rows, Z),
    )
    push, stress, thermal = pl.pallas_call(
        functools.partial(finish, Y * Z * nx * ny * nzd), out_shape=outs, in_specs=[spec] * 2, out_specs=(spec, spec, spec)
    )(*[pltpu.with_memory_space_constraint(r, pltpu.VMEM) for r in results])
    return push.reshape(offset.shape), stress, thermal.reshape(1)


def solution(mesh):
    placed = (
        P(None, None, "gx", "gy", "gz"),
        P(None, None, "gx", "gy", "gz"),
        P("gx", "gy", "gz"),
        P(None, None, None, "gx", "gy", "gz"),
    )
    sizes = tuple(mesh.shape[a] for a in ("gx", "gy", "gz"))
    return jax.shard_map(
        functools.partial(per_device, sizes),
        mesh=mesh,
        in_specs=placed,
        out_specs=(P(None, None, "gx", "gy", "gz"), P(), P()),
        check_vma=False,
    )
```
